128 devices in a mesh: grp: 2 (over z_lo), patch: 64 (over x, z_hi, y, core).
Axes of the slice: x: 4, y: 4, z: 4 (z_hi: 2, z_lo: 2; z = z_hi * 2 + z_lo), core: 2. Of those that a mesh axis runs over, the one named last changes fastest.
Arguments:
- displace: float32 [2, 131072, 384], P('grp', 'patch'), may hold values from -6 to 6
- velocity: float32 [2, 131072, 384], P('grp', 'patch'), may hold values from -6 to 6
- ext_force: float32 [2, 131072, 384], P('grp', 'patch'), may hold values from -6 to 6
- inv_mass: float32 [2, 131072, 128], P('grp', 'patch'), may hold values from 0.1 to 6
- thickness: float32 [2, 131072, 128], P('grp', 'patch'), may hold values from 0.5 to 2
- stiff_bands: bfloat16 [5, 384, 384], replicated, may hold values from -0.125 to 0.125
- pair_points: int32 [2, 64, 3, 1536], P('grp', 'patch'), may hold values from 0 to 6143
- pair_weights: float32 [2, 64, 3, 1536], P('grp', 'patch'), may hold values from 0.25 to 1
Outputs:
- displace_new: float32 [2, 131072, 384], P('grp', 'patch')
- velocity_new: float32 [2, 131072, 384], P('grp', 'patch')
The draws below stay inside these ranges and needn't reach their ends.
Inputs may be any that keep to these rules, and one draw needn't show every extreme that they name: `pair_points`: entry e names the control point in row e // 3 of the sending block (rows counted within the block) and point e % 3 across the strip.
All inputs are finite; a program needn't handle non-finite values.
Results may differ from the reference program's by a relative error of at most 0.00094.
The reference program's roundings to bfloat16 on the way count: a program that leaves them out, or rounds other values in their place, can miss the bound.
Values may be sent and summed in bfloat16 or wider, within the bound.
No kernel may reach another device: no remote copies, remote signals or barrier semaphores. Data moves between devices by JAX's collectives and lax.ppermute only.
A program may use at most 192 MiB of HBM per device.

```python
import math
import jax
import jax.numpy as jnp
from jax import lax

POINTS = 128
REACH = 2
SUBSTEPS = 4
TILES_DEV = 2048
SLOTS = 1536
ROW = 384
EDGE = 3
TILES = 131072
N_PATCH = 64


def draw_inv_mass(key, part):
    key_base, key_block, key_point = jax.random.split(jax.random.fold_in(key, 7), 3)
    block_total = 2 * N_PATCH
    position = jnp.arange(block_total, dtype=jnp.float32) / (block_total - 1)
    jitter = jax.random.uniform(key_block, (block_total,), jnp.float32, -0.05, 0.05)
    start = jax.random.uniform(key_base, (), jnp.float32, math.log(1.2), math.log(1.6))
    ceiling = jnp.exp(start + position * math.log(3.0) + jitter)
    per_row = jnp.repeat(ceiling.reshape(2, N_PATCH), TILES_DEV, axis=1)
    falling = jax.random.uniform(key_point, (2, TILES_DEV * N_PATCH, POINTS), jnp.float32, 0.0, math.log(4.0))
    return (per_row[:, :, None] * jnp.exp(-falling)).astype(jnp.float32)


def set_ends(drawn, rng, low, top_value):
    dims = drawn.shape
    place = [jax.random.randint(jax.random.fold_in(rng, axis), (), 0, dims[axis]) for axis in range(len(dims))]
    drawn = drawn.at[tuple(place)].set(low)
    longest = dims.index(max(dims))
    place[longest] = (place[longest] + 1) % dims[longest]
    return drawn.at[tuple(place)].set(top_value)


def block_scale(own_key, extent, cuts, low, top_value):
    loudness = 1.0
    for dim, shards_of in cuts:
        draws = jax.random.uniform(jax.random.fold_in(jax.random.fold_in(own_key, 6), dim), (shards_of,), jnp.float32, low / len(cuts), top_value / len(cuts))
        loudness = loudness * jnp.repeat(jnp.exp(draws), extent[dim] // shards_of).reshape((-1,) + (1,) * (len(extent) - 1 - dim))
    return loudness


def noise(key, shape, scale, limit, pieces=(), held_as=jnp.bfloat16):
    loudness = block_scale(key, shape, pieces, -0.22, 0.18) if pieces else 1.0
    array = jax.random.normal(key, shape, jnp.float32) * scale * loudness
    return jnp.minimum(jnp.maximum(array, -limit), limit).astype(held_as)


def setup_inputs(seed: int = 0) -> dict:
    seeds = jax.random.split(jax.random.key(seed), 9)
    displace = noise(seeds[0], (2, TILES, ROW), 1.0, 6.0, ((0, 2), (1, 64)), jnp.float32)
    velocity = noise(seeds[1], (2, TILES, ROW), 1.0, 6.0, ((0, 2), (1, 64)), jnp.float32)
    ext_force = noise(seeds[2], (2, TILES, ROW), 1.0, 6.0, ((0, 2), (1, 64)), jnp.float32)
    inv_mass = draw_inv_mass(jax.random.fold_in(seeds[8], 71), 0)
    thickness = jnp.clip(jnp.exp(math.log(2.0) - 1.3862944 * jax.random.uniform(seeds[4], (2, TILES, POINTS), jnp.float32) ** block_scale(seeds[4], (2, TILES, POINTS), ((0, 2), (1, 64)), -0.2, 0.2)), 0.5, 2.0)
    stiff_bands = noise(seeds[5], (2 * REACH + 1, ROW, ROW), ((2 * REACH + 1) * ROW) ** -0.5, 0.125)
    pair_points = set_ends(jax.random.randint(seeds[6], (2, N_PATCH, 3, SLOTS), 0, TILES_DEV * EDGE), jax.random.fold_in(seeds[6], 1), 0, (TILES_DEV * EDGE) - 1).astype(jnp.int32)
    pair_weights = jnp.clip(jnp.exp(math.log(1.0) - 1.3862944 * jax.random.uniform(seeds[7], (2, N_PATCH, 3, SLOTS), jnp.float32) ** block_scale(seeds[7], (2, N_PATCH, 3, SLOTS), ((0, 2), (1, 64)), -0.2, 0.2)), 0.25, 1.0)
    return dict(displace=displace, velocity=velocity, ext_force=ext_force, inv_mass=inv_mass, thickness=thickness, stiff_bands=stiff_bands, pair_points=pair_points, pair_weights=pair_weights)


PENALTY = 1.0
DAMPING = 0.5
COURANT = 0.4

def band_force(field, thickness, stiff_bands):
    row_count = field.shape[0]
    operand = lax.optimization_barrier(field.astype(jnp.bfloat16)).astype(jnp.float32)
    padded = jnp.pad(operand, ((REACH, REACH), (0, 0)))
    summed = jnp.zeros((row_count, 3 * POINTS), jnp.float32)
    for band_index in range(2 * REACH + 1):
        summed = summed + jnp.dot(padded[band_index:band_index + row_count], stiff_bands[band_index].astype(jnp.float32), precision=lax.Precision.HIGHEST)
    return (summed.reshape(row_count, 3, POINTS) * thickness[:, None, :]).reshape(row_count, 3 * POINTS)

def reference(displace, velocity, ext_force, inv_mass, thickness, stiff_bands, pair_points, pair_weights):
    row_width = 3 * POINTS
    base_step = COURANT * jnp.min(1.0 / jnp.sqrt(inv_mass * thickness))
    forces = [band_force(displace[group_index], thickness[group_index], stiff_bands) for group_index in range(2)]
    patch_base = (jnp.arange(N_PATCH, dtype=jnp.int32) * (TILES_DEV * row_width))[:, None, None]
    comp_offset = (jnp.arange(3, dtype=jnp.int32) * POINTS)[:, None, None, None]
    traces = []
    indices = []
    for group_index in range(2):
        pair_table = pair_points[group_index]
        flat_index = patch_base + pair_table // EDGE * row_width + pair_table % EDGE
        flat_index = (flat_index[None] + comp_offset).astype(jnp.int32)
        gathered = jnp.stack([displace[group_index].reshape(-1)[flat_index], velocity[group_index].reshape(-1)[flat_index], forces[group_index].reshape(-1)[flat_index]])
        traces.append(gathered)
        indices.append(flat_index)
    neighbour = (jnp.arange(N_PATCH, dtype=jnp.int32)[:, None] + jnp.arange(3, dtype=jnp.int32)[None, :] - 1).astype(jnp.int32)
    present = ((neighbour >= 0) & (neighbour < N_PATCH)).astype(jnp.float32)
    clipped = jnp.clip(neighbour, 0, N_PATCH - 1).astype(jnp.int32)
    mirror = jnp.broadcast_to((2 - jnp.arange(3, dtype=jnp.int32))[None, :], (N_PATCH, 3)).astype(jnp.int32)
    results_disp = []
    results_vel = []
    for group_index in range(2):
        gathered = traces[group_index]
        partner = traces[1 - group_index][:, :, clipped, mirror, :]
        weight = pair_weights[group_index] * present[:, :, None]
        slot_force = weight[None] * (-PENALTY * (gathered[0] - partner[0]) - DAMPING * (gathered[1] - partner[1]) + 0.5 * (partner[2] - gathered[2]))
        coupling = jnp.zeros((TILES * row_width,), jnp.float32).at[indices[group_index].reshape(-1)].add(slot_force.reshape(-1)).reshape(TILES, row_width)
        field = displace[group_index]
        moving = velocity[group_index]
        if group_index == 0:
            step_count = 1
            step_size = SUBSTEPS * base_step
        else:
            step_count = SUBSTEPS
            step_size = base_step
        for substep in range(step_count):
            if substep == 0:
                inner_force = forces[group_index]
            else:
                inner_force = band_force(field, thickness[group_index], stiff_bands)
            accel_now = ((ext_force[group_index] + coupling - inner_force).reshape(TILES, 3, POINTS) * inv_mass[group_index][:, None, :]).reshape(TILES, row_width)
            moving = moving + step_size * accel_now
            field = field + step_size * moving
        results_disp.append(field)
        results_vel.append(moving)
    return (jnp.stack(results_disp), jnp.stack(results_vel))
```

```python
import jax
import jax.numpy as jnp
from jax import lax
from jax.experimental import pallas as pl
from jax.experimental.pallas import tpu as pltpu
from jax.sharding import PartitionSpec as P

POINTS = 128
REACH = 2
SUBSTEPS = 4
EDGE = 3
COURANT = 0.4
ROWS = 2048
ROW = 384
SLOTS = 1536
HALO = 8
RUN = 129
PAIRS = 65
PLANE = 2080
TOP = 8
PAIR_ROWS = PAIRS * 16
BAND_ROWS = (PAIRS + 2) * 16
CHUNK = 208
F32 = jnp.float32
BF16 = jnp.bfloat16


def dot(a, b):
    return jnp.dot(a, b, preferred_element_type=F32)


def dot_nt(a, b):
    return lax.dot_general(a, b, (((1,), (1,)), ((), ())), preferred_element_type=F32)


def cols(c):
    return slice(c * 128, (c + 1) * 128)


def band_copies(stiff, wide_a, wide_b, wide_c, sem):
    copies = []
    for b in range(5):
        rows = pl.ds(b * ROW, ROW)
        next_rows = pl.ds((b + 1) * ROW, ROW)
        copies.append((stiff.at[b, :, pl.ds(0, 256)], wide_a.at[rows, :]))
        copies.append((stiff.at[b, :, pl.ds(256, 128)], wide_b.at[rows, pl.ds(0, 128)]))
        copies.append((stiff.at[b, :, pl.ds(0, 128)], wide_b.at[next_rows, pl.ds(128, 128)]))
        copies.append((stiff.at[b, :, pl.ds(128, 256)], wide_c.at[rows, :]))
    return [pltpu.make_async_copy(src, dst, sem.at[i]) for i, (src, dst) in enumerate(copies)]


def band_zeros(wide_b):
    wide_b[5 * ROW : 6 * ROW, 0:128] = jnp.zeros((ROW, 128), BF16)
    wide_b[0:ROW, 128:256] = jnp.zeros((ROW, 128), BF16)


def band_products(operand, start, wide_a, wide_b, wide_c):
    parts = [operand[i % 2, pl.ds(start + (i // 2) * 16, CHUNK), :] for i in range(6)]
    part_a = dot(jnp.concatenate(parts[:5], axis=1), wide_a[...])
    part_b = dot(jnp.concatenate(parts, axis=1), wide_b[...])
    part_c = dot(jnp.concatenate(parts[1:], axis=1), wide_c[...])
    even = [part_a[:, 0:128], part_a[:, 128:256], part_b[:, 0:128]]
    odd = [part_b[:, 128:256], part_c[:, 0:128], part_c[:, 128:256]]
    return even, odd


def plane_copies(array, halo_top, halo_bottom, plane, first, count, sem):
    copies = []
    for c in range(count):
        column = pl.ds(c * 128, 128)
        from_column = pl.ds(first + c * 128, 128)
        copies.append((array.at[0, :, column], plane.at[c, pl.ds(TOP + HALO, ROWS), :]))
        copies.append((halo_top.at[:, from_column], plane.at[c, pl.ds(TOP, HALO), :]))
        copies.append((halo_bottom.at[:, from_column], plane.at[c, pl.ds(TOP + HALO + ROWS, HALO), :]))
    return [pltpu.make_async_copy(src, dst, sem.at[i]) for i, (src, dst) in enumerate(copies)]


def clear_ends(plane, count):
    for c in range(count):
        plane[c, 0:TOP, :] = jnp.zeros((TOP, 128), F32)
        plane[c, PLANE - 8 : PLANE, :] = jnp.zeros((8, 128), F32)


def spread(k):
    return pl.ds(TOP + k, 16, stride=RUN)


def first_kernel(
    displace, velocity, thickness, stiff, halo_top, halo_bottom, points,
    force, compact, send_0, send_1, send_2,
    field, moving, thick, operand, force_vmem, wide_a, wide_b, wide_c, table,
    sem_field, sem_moving, sem_thick, sem_band, sem_out,
):
    field_in = plane_copies(displace, halo_top, halo_bottom, field, 0, 3, sem_field)
    moving_in = plane_copies(velocity, halo_top, halo_bottom, moving, 384, 3, sem_moving)
    thick_in = plane_copies(thickness, halo_top, halo_bottom, thick, 1280, 1, sem_thick)
    bands_in = band_copies(stiff, wide_a, wide_b, wide_c, sem_band)
    for copy in field_in + bands_in + moving_in + thick_in:
        copy.start()
    clear_ends(field, 3)
    clear_ends(moving, 3)
    clear_ends(thick, 1)
    band_zeros(wide_b)
    for copy in field_in:
        copy.wait()

    def make_operand(step, carry):
        for half in range(2):
            for c in range(3):
                operand[half, pl.ds(pl.multiple_of(step * 16, 16), 16), cols(c)] = field[
                    c, spread(2 * step + half - 2), :
                ].astype(BF16)
        return carry

    lax.fori_loop(0, PAIRS + 2, make_operand, 0)
    for copy in bands_in:
        copy.wait()
    force_out = []
    for chunk in range(PAIR_ROWS // CHUNK):
        start = chunk * CHUNK
        results = band_products(operand, start, wide_a, wide_b, wide_c)
        for half in range(2):
            for c in range(3):
                force_vmem[half, start : start + CHUNK, cols(c)] = results[half][c]
    for half in range(2):
        force_out.append(pltpu.make_async_copy(force_vmem.at[half], force.at[half], sem_out.at[half]))
    for copy in force_out:
        copy.start()
    for copy in moving_in + thick_in:
        copy.wait()
    lane = lax.broadcasted_iota(jnp.int32, (16, 128), 1)

    def make_compact(step, carry):
        for half in range(2):
            at = spread(2 * step + half)
            half_thick = 0.5 * thick[0, at, :]
            parts = [
                field[c, at, :]
                + 0.5 * moving[c, at, :]
                + half_thick * force_vmem[half, pl.ds(pl.multiple_of(step * 16, 16), 16), cols(c)]
                for c in range(3)
            ]
            compact[at, :] = jnp.where(
                lane < 3,
                parts[0],
                jnp.where(lane < 6, pltpu.roll(parts[1], 3, 1), pltpu.roll(parts[2], 6, 1)),
            )
        return carry

    lax.fori_loop(0, PAIRS, make_compact, 0)
    for group in range(16):
        start = TOP + HALO + group * 128
        turned = compact[start : start + 128, :].T[0:16, :]
        high = turned.astype(BF16)
        table[group * 16 : group * 16 + 16, 0:128] = high
        table[group * 16 : group * 16 + 16, 128:256] = (turned - high.astype(F32)).astype(BF16)
    place = lax.broadcasted_iota(jnp.int32, (128, SLOTS), 0)
    for j, send in enumerate([send_0, send_1, send_2]):
        entry = points[j : j + 1, :]
        row = (entry * 21846) >> 16
        point = entry - 3 * row
        low = row & 127
        group_of = row >> 7
        chosen = jnp.where(place == low, 1.0, 0.0).astype(BF16)
        picked = dot(table[...], jnp.concatenate([chosen, chosen], axis=0))
        total = jnp.zeros((16, SLOTS), F32)
        for group in range(16):
            total = total + jnp.where(group_of == group, picked[group * 16 : group * 16 + 16, :], 0.0)
        for c in range(3):
            value = jnp.where(
                point == 0,
                total[3 * c : 3 * c + 1, :],
                jnp.where(point == 1, total[3 * c + 1 : 3 * c + 2, :], total[3 * c + 2 : 3 * c + 3, :]),
            )
            send[c : c + 1, :] = value
    for copy in force_out:
        copy.wait()


def couple_kernel(where_am_i, got_0, got_1, got_2, points, weights, compact, coupling, edge_top, edge_bottom, total):
    block = where_am_i[1]
    blocks = where_am_i[2]
    place = lax.broadcasted_iota(jnp.int32, (128, SLOTS), 0)
    line = lax.broadcasted_iota(jnp.int32, (16, SLOTS), 0)
    summed = None
    for j, got in enumerate([got_0, got_1, got_2]):
        entry = points[j : j + 1, :]
        row = (entry * 21846) >> 16
        point = entry - 3 * row
        low = row & 127
        group_of = row >> 7
        neighbour = block + (j - 1)
        present = jnp.where((neighbour >= 0) & (neighbour < blocks), 1.0, 0.0)
        weight = weights[j : j + 1, :] * present
        spread_out = jnp.zeros((16, SLOTS), F32)
        for c in range(4):
            value = weight * got[c : c + 1, :] if c < 3 else weight
            spread_out = jnp.where(line == 3 * c + point, value, spread_out)
        high = spread_out.astype(BF16)
        rest = (spread_out - high.astype(F32)).astype(BF16)
        zero = jnp.zeros((16, SLOTS), BF16)
        right = jnp.concatenate(
            [jnp.where(group_of == group, high, zero) for group in range(16)]
            + [jnp.where(group_of == group, rest, zero) for group in range(16)],
            axis=0,
        )
        chosen = jnp.where(place == low, 1.0, 0.0).astype(BF16)
        part = dot_nt(chosen, right)
        summed = part if summed is None else summed + part
    total[...] = summed[:, 0:256] + summed[:, 256:512]
    lane = lax.broadcasted_iota(jnp.int32, (128, 128), 1)
    for group in range(16):
        half = total[:, (group // 8) * 128 : (group // 8) * 128 + 128]
        shift = (group % 8) * 16
        block_sum = pltpu.roll(half, 128 - shift, 1) if shift else half
        weight_sum = jnp.where(
            lane < 3,
            pltpu.roll(block_sum, 119, 1),
            jnp.where(lane < 6, pltpu.roll(block_sum, 122, 1), pltpu.roll(block_sum, 125, 1)),
        )
        start = TOP + HALO + group * 128
        here = block_sum - compact[start : start + 128, :] * weight_sum
        here = jnp.where(lane < 9, here, 0.0)
        coupling[group * 128 : group * 128 + 128, :] = here
        if group == 0:
            edge_top[...] = here[0:8, :]
        if group == 15:
            edge_bottom[...] = here[120:128, :]


def step_kernel(
    where_am_i, stiffest, displace, velocity, ext_force, inv_mass, thickness, stiff, halo_top, halo_bottom,
    force, coupling, couple_top, couple_bottom,
    new_field, new_moving,
    field, moving, outer, mass, thick, couple, force_vmem,
    state, speed, push, drag, operand_a, operand_b, wide_a, wide_b, wide_c,
    sem_field, sem_moving, sem_outer, sem_mass, sem_thick, sem_couple, sem_force, sem_band, sem_out,
):
    fine = where_am_i[0] == 1
    arrays = [
        plane_copies(displace, halo_top, halo_bottom, field, 0, 3, sem_field),
        plane_copies(velocity, halo_top, halo_bottom, moving, 384, 3, sem_moving),
        plane_copies(ext_force, halo_top, halo_bottom, outer, 768, 3, sem_outer),
        plane_copies(inv_mass, halo_top, halo_bottom, mass, 1152, 1, sem_mass),
        plane_copies(thickness, halo_top, halo_bottom, thick, 1280, 1, sem_thick),
    ]
    arrays.append(
        [
            pltpu.make_async_copy(coupling, couple.at[pl.ds(TOP + HALO, ROWS), :], sem_couple.at[0]),
            pltpu.make_async_copy(couple_top, couple.at[pl.ds(TOP, HALO), :], sem_couple.at[1]),
            pltpu.make_async_copy(couple_bottom, couple.at[pl.ds(TOP + HALO + ROWS, HALO), :], sem_couple.at[2]),
            pltpu.make_async_copy(force, force_vmem, sem_force.at[0]),
        ]
    )
    bands_in = band_copies(stiff, wide_a, wide_b, wide_c, sem_band)
    for group in arrays + [bands_in]:
        for copy in group:
            copy.start()
    clear_ends(field, 3)
    clear_ends(moving, 3)
    clear_ends(outer, 3)
    clear_ends(mass, 1)
    clear_ends(thick, 1)
    couple[PLANE - 8 : PLANE, :] = jnp.zeros((8, 128), F32)
    band_zeros(wide_b)
    limit = jnp.full((16, 128), stiffest[0], F32)
    base_step = COURANT * (1.0 / jnp.sqrt(limit))
    size = jnp.where(fine, base_step, SUBSTEPS * base_step)
    square = size * size
    for group in arrays:
        for copy in group:
            copy.wait()
    lane = lax.broadcasted_iota(jnp.int32, (16, 128), 1)

    def first_step(step, carry):
        for half in range(2):
            at = spread(2 * step + half)
            tile = pl.ds(pl.multiple_of(step * 16, 16), 16)
            next_tile = pl.ds(pl.multiple_of(step * 16 + 16, 16), 16)
            scaled = square * mass[0, at, :]
            pull = scaled * thick[0, at, :]
            drag[half, tile, :] = pull
            both = couple[at, :]
            for c in range(3):
                here = jnp.where(lane < 3, pltpu.roll(both, 128 - 3 * c, 1) if c else both, 0.0)
                drive = scaled * (outer[c, at, :] + here)
                push[half, tile, cols(c)] = drive
                new_speed = size * moving[c, at, :] + (drive - pull * force_vmem[half, tile, cols(c)])
                place = field[c, at, :] + new_speed
                speed[half, tile, cols(c)] = new_speed
                state[half, tile, cols(c)] = place
                operand_a[half, next_tile, cols(c)] = place.astype(BF16)
        return carry

    lax.fori_loop(0, PAIRS, first_step, 0)
    for copy in bands_in:
        copy.wait()

    def fill_ends(operand):
        for c in range(3):
            operand[0, 0:16, cols(c)] = pltpu.roll(state[1, 63 * 16 : 64 * 16, cols(c)], 1, 0).astype(BF16)
            operand[1, 0:16, cols(c)] = pltpu.roll(state[0, 64 * 16 : 65 * 16, cols(c)], 1, 0).astype(BF16)
            operand[0, 66 * 16 : 67 * 16, cols(c)] = pltpu.roll(state[1, 0:16, cols(c)], 15, 0).astype(BF16)
            operand[1, 66 * 16 : 67 * 16, cols(c)] = pltpu.roll(state[0, 16:32, cols(c)], 15, 0).astype(BF16)

    def substep(operand, following):
        def update(start, results):
            rows = slice(start, start + CHUNK)
            for half in range(2):
                pull = drag[half, rows, :]
                for c in range(3):
                    new_speed = speed[half, rows, cols(c)] + (push[half, rows, cols(c)] - pull * results[half][c])
                    place = state[half, rows, cols(c)] + new_speed
                    speed[half, rows, cols(c)] = new_speed
                    state[half, rows, cols(c)] = place
                    if following is not None:
                        following[half, start + 16 : start + 16 + CHUNK, cols(c)] = place.astype(BF16)

        before = None
        for chunk in range(PAIR_ROWS // CHUNK):
            start = chunk * CHUNK
            results = band_products(operand, start, wide_a, wide_b, wide_c)
            if before is not None:
                update(*before)
            before = (start, results)
        update(*before)

    @pl.when(fine)
    def _():
        fill_ends(operand_a)
        substep(operand_a, operand_b)
        fill_ends(operand_b)
        substep(operand_b, operand_a)
        fill_ends(operand_a)
        substep(operand_a, None)

    inverse = 1.0 / size

    def last(step, carry):
        for half in range(2):
            at = spread(2 * step + half)
            tile = pl.ds(pl.multiple_of(step * 16, 16), 16)
            for c in range(3):
                field[c, at, :] = state[half, tile, cols(c)]
                moving[c, at, :] = speed[half, tile, cols(c)] * inverse
        return carry

    lax.fori_loop(0, PAIRS, last, 0)
    out = []
    for c in range(3):
        inner = pl.ds(TOP + HALO, ROWS)
        out.append(pltpu.make_async_copy(field.at[c, inner, :], new_field.at[0, :, pl.ds(c * 128, 128)], sem_out.at[c]))
        out.append(
            pltpu.make_async_copy(moving.at[c, inner, :], new_moving.at[0, :, pl.ds(c * 128, 128)], sem_out.at[3 + c])
        )
    for copy in out:
        copy.start()
    for copy in out:
        copy.wait()


ANY = pl.BlockSpec(memory_space=pl.ANY)
IN_VMEM = pl.BlockSpec(memory_space=pltpu.VMEM)
IN_SMEM = pl.BlockSpec(memory_space=pltpu.SMEM)
DMA = pltpu.SemaphoreType.DMA


def shape(*dims):
    return jax.ShapeDtypeStruct(dims, F32)


def per_device(
    displace, velocity, ext_force, inv_mass, thickness, stiff_bands, pair_points, pair_weights
):
    group = lax.axis_index("grp")
    block = lax.axis_index("patch")
    blocks = lax.axis_size("patch")
    where_am_i = jnp.stack([group, block, jnp.int32(blocks)]).astype(jnp.int32)
    points = pair_points[0, 0]
    weights = pair_weights[0, 0]
    down = [(i, i + 1) for i in range(blocks - 1)]
    up = [(i + 1, i) for i in range(blocks - 1)]
    arrays = [displace, velocity, ext_force, inv_mass, thickness]
    first_rows = jnp.concatenate([a[0, :HALO] for a in arrays], axis=1)
    last_rows = jnp.concatenate([a[0, ROWS - HALO :] for a in arrays], axis=1)
    halo_top = lax.ppermute(last_rows, "patch", down)
    halo_bottom = lax.ppermute(first_rows, "patch", up)
    local = jnp.broadcast_to(jnp.max(inv_mass * thickness), (2 * blocks, 1, 128))
    stiffest = jnp.max(lax.all_to_all(local, ("grp", "patch"), 0, 0)).reshape(1)

    bands = [
        pltpu.VMEM((5 * ROW, 256), BF16),
        pltpu.VMEM((6 * ROW, 256), BF16),
        pltpu.VMEM((5 * ROW, 256), BF16),
    ]
    plane_3 = pltpu.VMEM((3, PLANE, 128), F32)
    plane_1 = pltpu.VMEM((1, PLANE, 128), F32)
    full = pltpu.VMEM((2, PAIR_ROWS, ROW), F32)
    band_operand = pltpu.VMEM((2, BAND_ROWS, ROW), BF16)
    force, compact, send_0, send_1, send_2 = pl.pallas_call(
        first_kernel,
        out_shape=(
            shape(2, PAIR_ROWS, ROW),
            shape(PLANE, 128),
            shape(3, SLOTS),
            shape(3, SLOTS),
            shape(3, SLOTS),
        ),
        in_specs=[ANY] * 6 + [IN_VMEM],
        out_specs=[ANY] + [IN_VMEM] * 4,
        scratch_shapes=[plane_3, plane_3, plane_1, band_operand, full]
        + bands
        + [pltpu.VMEM((256, 256), BF16)]
        + [DMA((9,)), DMA((9,)), DMA((3,)), DMA((20,)), DMA((2,))],
        name="first_force",
    )(displace, velocity, thickness, stiff_bands, halo_top, halo_bottom, points)

    both = ("grp", "patch")
    got = []
    sends = [send_0, send_1, send_2]
    for j in range(3):
        pairs = []
        for g in range(2):
            for p in range(blocks):
                target = p + 1 - j
                if 0 <= target < blocks:
                    pairs.append((g * blocks + p, (1 - g) * blocks + target))
        got.append(lax.ppermute(sends[2 - j], both, pairs))

    coupling, edge_top, edge_bottom = pl.pallas_call(
        couple_kernel,
        out_shape=(shape(ROWS, 128), shape(8, 128), shape(8, 128)),
        in_specs=[IN_SMEM] + [IN_VMEM] * 6,
        out_specs=[IN_VMEM] * 3,
        scratch_shapes=[pltpu.VMEM((128, 256), F32)],
        name="couple",
    )(where_am_i, *got, points, weights, compact)
    couple_top = lax.ppermute(edge_bottom, "patch", down)
    couple_bottom = lax.ppermute(edge_top, "patch", up)

    new_field, new_moving = pl.pallas_call(
        step_kernel,
        out_shape=(shape(1, ROWS, ROW), shape(1, ROWS, ROW)),
        in_specs=[IN_SMEM] * 2 + [ANY] * 12,
        out_specs=[ANY] * 2,
        scratch_shapes=[plane_3, plane_3, plane_3, plane_1, plane_1, pltpu.VMEM((PLANE, 128), F32), full]
        + [full, full, full, pltpu.VMEM((2, PAIR_ROWS, 128), F32)]
        + [band_operand, band_operand]
        + bands
        + [DMA((9,)), DMA((9,)), DMA((9,)), DMA((3,)), DMA((3,)), DMA((3,)), DMA((1,)), DMA((20,)), DMA((6,))],
        name="steps",
    )(
        where_am_i, stiffest, displace, velocity, ext_force, inv_mass, thickness, stiff_bands,
        halo_top, halo_bottom, force, coupling, couple_top, couple_bottom,
    )
    return new_field, new_moving


def solution(mesh):
    spec3 = P("grp", "patch", None)
    spec4 = P("grp", "patch", None, None)
    return jax.shard_map(
        per_device,
        mesh=mesh,
        in_specs=(spec3, spec3, spec3, spec3, spec3, P(), spec4, spec4),
        out_specs=(spec3, spec3),
        check_vma=False,
    )
```

```python
import jax
import jax.numpy as jnp
from jax import lax
from jax.experimental import pallas as pl
from jax.experimental.pallas import tpu as pltpu
from jax.sharding import PartitionSpec as P

POINTS = 128
REACH = 2
SUBSTEPS = 4
EDGE = 3
COURANT = 0.4
ROWS = 2048
ROW = 384
SLOTS = 1536
HALO = 8
RUN = 129
PAIRS = 65
PLANE = 2080
TOP = 8
PAIR_ROWS = PAIRS * 16
BAND_ROWS = (PAIRS + 2) * 16
CHUNK = 208
CHUNK_PAIRS = CHUNK // 16
F32 = jnp.float32
BF16 = jnp.bfloat16


def dot(a, b):
    return jnp.dot(a, b, preferred_element_type=F32)


def dot_nt(a, b):
    return lax.dot_general(a, b, (((1,), (1,)), ((), ())), preferred_element_type=F32)


def cols(c):
    return slice(c * 128, (c + 1) * 128)


def band_copies(stiff, wide_a, wide_b, wide_c, sem):
    copies = []
    for b in range(5):
        rows = pl.ds(b * ROW, ROW)
        next_rows = pl.ds((b + 1) * ROW, ROW)
        copies.append((stiff.at[b, :, pl.ds(0, 256)], wide_a.at[rows, :]))
        copies.append((stiff.at[b, :, pl.ds(256, 128)], wide_b.at[rows, pl.ds(0, 128)]))
        copies.append((stiff.at[b, :, pl.ds(0, 128)], wide_b.at[next_rows, pl.ds(128, 128)]))
        copies.append((stiff.at[b, :, pl.ds(128, 256)], wide_c.at[rows, :]))
    return [pltpu.make_async_copy(src, dst, sem.at[i]) for i, (src, dst) in enumerate(copies)]


def band_zeros(wide_b):
    wide_b[5 * ROW : 6 * ROW, 0:128] = jnp.zeros((ROW, 128), BF16)
    wide_b[0:ROW, 128:256] = jnp.zeros((ROW, 128), BF16)


def band_products(operand, start, wide_a, wide_b, wide_c):
    parts = [operand[i % 2, pl.ds(start + (i // 2) * 16, CHUNK), :] for i in range(6)]
    part_a = dot(jnp.concatenate(parts[:5], axis=1), wide_a[...])
    part_b = dot(jnp.concatenate(parts, axis=1), wide_b[...])
    part_c = dot(jnp.concatenate(parts[1:], axis=1), wide_c[...])
    even = [part_a[:, 0:128], part_a[:, 128:256], part_b[:, 0:128]]
    odd = [part_b[:, 128:256], part_c[:, 0:128], part_c[:, 128:256]]
    return even, odd


def put_halo(plane, near, far, even, first, count):
    for c in range(count):
        column = slice(first + c * 128, first + c * 128 + 128)
        plane[c, TOP : TOP + HALO, :] = jnp.where(even, far[:, column], near[:, column])
        plane[c, TOP + HALO + ROWS : TOP + 2 * HALO + ROWS, :] = jnp.where(even, near[:, column], far[:, column])
        plane[c, 0:TOP, :] = jnp.zeros((TOP, 128), F32)
        plane[c, PLANE - 8 : PLANE, :] = jnp.zeros((8, 128), F32)


def plane_copies(array, plane, count, sem):
    return [
        pltpu.make_async_copy(
            array.at[0, :, pl.ds(c * 128, 128)], plane.at[c, pl.ds(TOP + HALO, ROWS), :], sem.at[c]
        )
        for c in range(count)
    ]


def spread(k):
    return pl.ds(TOP + k, 16, stride=RUN)


def bundle_kernel(displace, velocity, ext_force, inv_mass, thickness, near_rows, far_rows, sem):
    even = lax.axis_index("patch") % 2 == 0
    copies = []
    last = ROWS - HALO
    near_start = pl.multiple_of(jnp.where(even, last, 0), 8)
    far_start = pl.multiple_of(jnp.where(even, 0, last), 8)
    column = 0
    for array in [displace, velocity, ext_force, inv_mass, thickness]:
        width = array.shape[2]
        for rows, out in [(far_start, far_rows), (near_start, near_rows)]:
            copies.append(
                pltpu.make_async_copy(
                    array.at[0, pl.ds(rows, HALO), :], out.at[:, pl.ds(column, width)], sem.at[len(copies)]
                )
            )
        column += width
    for copy in copies:
        copy.start()
    for copy in copies:
        copy.wait()


def fill_operand(field, operand, step):
    for half in range(2):
        for c in range(3):
            operand[half, pl.ds(step * 16, 16), cols(c)] = field[c, spread(2 * step + half - 2), :].astype(BF16)


def load_kernel(displace, stiff, field, operand, wide_a, wide_b, wide_c, sem_field, sem_band):
    field_in = plane_copies(displace, field, 3, sem_field)
    bands_in = band_copies(stiff, wide_a, wide_b, wide_c, sem_band)
    for copy in field_in + bands_in:
        copy.start()
    for c in range(3):
        field[c, 0 : TOP + HALO, :] = jnp.zeros((TOP + HALO, 128), F32)
        field[c, TOP + HALO + ROWS : PLANE, :] = jnp.zeros((PLANE - TOP - HALO - ROWS, 128), F32)
    band_zeros(wide_b)
    for copy in field_in:
        copy.wait()

    def some(i, carry):
        for j in range(4):
            fill_operand(field, operand, pl.multiple_of(i * 4, 4) + j + 3)
        return carry

    for step in range(3):
        fill_operand(field, operand, step)
    lax.fori_loop(0, (PAIRS - 1) // 4, some, 0)
    for copy in bands_in:
        copy.wait()


def slot_place(entry):
    row = (entry * 21846) >> 16
    return row >> 7, row & 127, entry - 3 * row


def first_kernel(
    field_in, operand_in, wide_a, wide_b, wide_c, near_rows, far_rows, points,
    velocity, ext_force, inv_mass, thickness,
    field, operand, moving, outer, mass, thick, force, compact, stiffest, send_far, send_mid, send_near,
    table, sem_moving, sem_outer, sem_mass, sem_thick,
):
    even = lax.axis_index("patch") % 2 == 0
    near_j = jnp.where(even, 2, 0)
    thick_in = plane_copies(thickness, thick, 1, sem_thick)
    moving_in = plane_copies(velocity, moving, 3, sem_moving)
    mass_in = plane_copies(inv_mass, mass, 1, sem_mass)
    outer_in = plane_copies(ext_force, outer, 3, sem_outer)
    for copy in thick_in + moving_in + mass_in + outer_in:
        copy.start()
    put_halo(field, near_rows, far_rows, even, 0, 3)
    put_halo(moving, near_rows, far_rows, even, 384, 3)
    put_halo(outer, near_rows, far_rows, even, 768, 3)
    put_halo(mass, near_rows, far_rows, even, 1152, 1)
    put_halo(thick, near_rows, far_rows, even, 1280, 1)
    for step in list(range(6)) + list(range(60, 67)):
        fill_operand(field, operand, step)
    lane = lax.broadcasted_iota(jnp.int32, (16, 128), 1)

    def make_compact(start, results):
        for i in range(CHUNK_PAIRS):
            for half in range(2):
                at = spread(2 * (start // 16 + i) + half)
                half_thick = 0.5 * thick[0, at, :]
                parts = [
                    field[c, at, :]
                    + 0.5 * moving[c, at, :]
                    + half_thick * results[half][c][i * 16 : i * 16 + 16, :]
                    for c in range(3)
                ]
                compact[at, :] = jnp.where(
                    lane < 3,
                    parts[0],
                    jnp.where(lane < 6, pltpu.roll(parts[1], 3, 1), pltpu.roll(parts[2], 6, 1)),
                )

    before = None
    for start in range(0, PAIR_ROWS, CHUNK):
        results = band_products(operand, start, wide_a, wide_b, wide_c)
        for half in range(2):
            for c in range(3):
                force[half, start : start + CHUNK, cols(c)] = results[half][c]
        if before is None:
            for copy in thick_in + moving_in:
                copy.wait()
        else:
            make_compact(*before)
        before = (start, results)
    make_compact(*before)
    for group in range(16):
        start = TOP + HALO + group * 128
        turned = compact[start : start + 128, :].T[0:16, :]
        high = turned.astype(BF16)
        table[group * 16 : group * 16 + 16, 0:128] = high
        table[group * 16 : group * 16 + 16, 128:256] = (turned - high.astype(F32)).astype(BF16)
    place = lax.broadcasted_iota(jnp.int32, (128, SLOTS), 0)
    for j, send in [(2 - near_j, send_far), (1, send_mid), (near_j, send_near)]:
        group_of, low, point = slot_place(points[j])
        chosen = jnp.where(place == low, 1.0, 0.0).astype(BF16)
        picked = dot(table[...], jnp.concatenate([chosen, chosen], axis=0))
        total = jnp.zeros((16, SLOTS), F32)
        for group in range(16):
            total = total + jnp.where(group_of == group, picked[group * 16 : group * 16 + 16, :], 0.0)
        for c in range(3):
            send[c] = jnp.where(
                point == 0,
                total[3 * c : 3 * c + 1, :],
                jnp.where(point == 1, total[3 * c + 1 : 3 * c + 2, :], total[3 * c + 2 : 3 * c + 3, :]),
            )
    for copy in mass_in:
        copy.wait()
    product = jnp.zeros((8, 128), F32)
    for i in range(8):
        rows = slice(TOP + HALO + i * 256, TOP + HALO + i * 256 + 256)
        product = jnp.maximum(
            product, jnp.max((mass[0, rows, :] * thick[0, rows, :]).reshape(32, 8, 128), axis=0)
        )
    stiffest[...] = product
    for copy in outer_in:
        copy.wait()


def couple_kernel(got_far, got_mid, got_near, points, weights, compact, stiffest, coupling, parcel, total):
    group_here = lax.axis_index("grp")
    block = lax.axis_index("patch")
    blocks = lax.axis_size("patch")
    place = lax.broadcasted_iota(jnp.int32, (128, SLOTS), 0)
    line = lax.broadcasted_iota(jnp.int32, (16, SLOTS), 0)
    summed = None
    near_j = jnp.where(block % 2 == 0, 2, 0)
    for j, got in [(2 - near_j, got_far), (1, got_mid), (near_j, got_near)]:
        group_of, low, point = slot_place(points[j])
        neighbour = block + (j - 1)
        present = jnp.where((neighbour >= 0) & (neighbour < blocks), 1.0, 0.0)
        weight = weights[j] * present
        spread_out = jnp.zeros((16, SLOTS), F32)
        for c in range(4):
            value = weight * got[c] if c < 3 else weight
            spread_out = jnp.where(line == 3 * c + point, value, spread_out)
        high = spread_out.astype(BF16)
        rest = (spread_out - high.astype(F32)).astype(BF16)
        zero = jnp.zeros((16, SLOTS), BF16)
        right = jnp.concatenate(
            [jnp.where(group_of == group, high, zero) for group in range(16)]
            + [jnp.where(group_of == group, rest, zero) for group in range(16)],
            axis=0,
        )
        chosen = jnp.where(place == low, 1.0, 0.0).astype(BF16)
        part = dot_nt(chosen, right)
        summed = part if summed is None else summed + part
    total[...] = summed[:, 0:256] + summed[:, 256:512]
    lane = lax.broadcasted_iota(jnp.int32, (128, 128), 1)
    edges = []
    for group in range(16):
        half = total[:, (group // 8) * 128 : (group // 8) * 128 + 128]
        shift = (group % 8) * 16
        block_sum = pltpu.roll(half, 128 - shift, 1) if shift else half
        weight_sum = jnp.where(
            lane < 3,
            pltpu.roll(block_sum, 119, 1),
            jnp.where(lane < 6, pltpu.roll(block_sum, 122, 1), pltpu.roll(block_sum, 125, 1)),
        )
        start = TOP + HALO + group * 128
        here = block_sum - compact[start : start + 128, :] * weight_sum
        here = jnp.where(lane < 9, here, 0.0)
        coupling[group * 128 : group * 128 + 128, :] = here
        if group == 0:
            edges.append(here[0:8, :])
        if group == 15:
            edges.append(here[120:128, :])
    lane_row = lax.broadcasted_iota(jnp.int32, (1, 128), 1)
    most = jnp.max(jnp.max(stiffest[...], axis=0, keepdims=True), axis=1, keepdims=True)
    flat = []
    for edge in edges:
        line_up = edge[0:1, :]
        for row in range(1, 8):
            line_up = line_up + pltpu.roll(edge, 16 * row, 1)[row : row + 1, :]
        flat.append(jnp.where(lane_row == 15, most, line_up))
    parcel[...] = jnp.broadcast_to(flat[0][None], (128, 1, 128))
    here_index = group_here * blocks + block
    parcel[jnp.minimum(here_index + 1, 2 * blocks - 1)] = flat[1]


def step_kernel(
    parcel, field, moving, outer, mass, thick, force, coupling, wide_a, wide_b, wide_c,
    new_field, new_moving,
    couple, state, speed, push, drag, operand_a, operand_b, place_out, speed_out, sem_out,
):
    group_here = lax.axis_index("grp")
    block = lax.axis_index("patch")
    blocks = lax.axis_size("patch")
    fine = group_here == 1
    lane_row = lax.broadcasted_iota(jnp.int32, (1, 128), 1)
    sublane = lax.broadcasted_iota(jnp.int32, (8, 128), 0)
    most = jnp.max(parcel[...].reshape(2 * blocks, 128), axis=0, keepdims=True)
    most = jnp.max(jnp.where(lane_row == 15, most, 0.0), axis=1, keepdims=True)
    limit = jnp.broadcast_to(most, (16, 128))
    base_step = COURANT * (1.0 / jnp.sqrt(limit))
    size = jnp.where(fine, base_step, SUBSTEPS * base_step)
    square = size * size
    inverse = 1.0 / size
    here_index = group_here * blocks + block
    for start, there, exists in [
        (TOP, jnp.maximum(here_index - 1, 0), block > 0),
        (TOP + HALO + ROWS, jnp.minimum(here_index + 1, 2 * blocks - 1), block < blocks - 1),
    ]:
        line_up = jnp.broadcast_to(parcel[there], (8, 128))
        edge = line_up
        for row in range(1, 8):
            edge = jnp.where(sublane == row, pltpu.roll(line_up, 128 - 16 * row, 1), edge)
        couple[start : start + 8, :] = jnp.where(exists, edge, 0.0)
    couple[TOP + HALO : TOP + HALO + ROWS, :] = coupling[...]
    couple[0:TOP, :] = jnp.zeros((TOP, 128), F32)
    couple[PLANE - 8 : PLANE, :] = jnp.zeros((8, 128), F32)
    lane = lax.broadcasted_iota(jnp.int32, (16, 128), 1)

    def first_step(turn, carry):
        for i in range(5):
            step = turn * 5 + i
            for half in range(2):
                at = spread(2 * step + half)
                tile = pl.ds(pl.multiple_of(step * 16, 16), 16)
                next_tile = pl.ds(pl.multiple_of(step * 16 + 16, 16), 16)
                scaled = square * mass[0, at, :]
                pull = scaled * thick[0, at, :]
                drag[half, tile, :] = pull
                both = couple[at, :]
                for c in range(3):
                    here = jnp.where(lane < 3, pltpu.roll(both, 128 - 3 * c, 1) if c else both, 0.0)
                    drive = scaled * (outer[c, at, :] + here)
                    push[half, tile, cols(c)] = drive
                    new_speed = size * moving[c, at, :] + (drive - pull * force[half, tile, cols(c)])
                    place = field[c, at, :] + new_speed
                    speed[half, tile, cols(c)] = new_speed
                    state[half, tile, cols(c)] = place
                    operand_a[half, next_tile, cols(c)] = place.astype(BF16)
        return carry

    lax.fori_loop(0, PAIRS // 5, first_step, 0)

    def fill_ends(operand):
        for c in range(3):
            operand[0, 0:16, cols(c)] = pltpu.roll(state[1, 63 * 16 : 64 * 16, cols(c)], 1, 0).astype(BF16)
            operand[1, 0:16, cols(c)] = pltpu.roll(state[0, 64 * 16 : 65 * 16, cols(c)], 1, 0).astype(BF16)
            operand[0, 66 * 16 : 67 * 16, cols(c)] = pltpu.roll(state[1, 0:16, cols(c)], 15, 0).astype(BF16)
            operand[1, 66 * 16 : 67 * 16, cols(c)] = pltpu.roll(state[0, 16:32, cols(c)], 15, 0).astype(BF16)

    def substep(operand, following):
        def update(start, results):
            rows = slice(start, start + CHUNK)
            for half in range(2):
                pull = drag[half, rows, :]
                for c in range(3):
                    new_speed = speed[half, rows, cols(c)] + (push[half, rows, cols(c)] - pull * results[half][c])
                    place = state[half, rows, cols(c)] + new_speed
                    if following is not None:
                        speed[half, rows, cols(c)] = new_speed
                        state[half, rows, cols(c)] = place
                        following[half, start + 16 : start + 16 + CHUNK, cols(c)] = place.astype(BF16)
                    else:
                        for i in range(CHUNK_PAIRS):
                            at = spread(2 * (start // 16 + i) + half)
                            place_out[c, at, :] = place[i * 16 : i * 16 + 16, :]
                            speed_out[c, at, :] = new_speed[i * 16 : i * 16 + 16, :] * inverse

        before = None
        for start in range(0, PAIR_ROWS, CHUNK):
            results = band_products(operand, start, wide_a, wide_b, wide_c)
            if before is not None:
                update(*before)
            before = (start, results)
        update(*before)

    @pl.when(fine)
    def _():
        fill_ends(operand_a)
        substep(operand_a, operand_b)
        fill_ends(operand_b)
        substep(operand_b, operand_a)
        fill_ends(operand_a)
        substep(operand_a, None)

    @pl.when(jnp.logical_not(fine))
    def _():
        def last(turn, carry):
            for i in range(5):
                step = turn * 5 + i
                for half in range(2):
                    at = spread(2 * step + half)
                    tile = pl.ds(pl.multiple_of(step * 16, 16), 16)
                    for c in range(3):
                        place_out[c, at, :] = state[half, tile, cols(c)]
                        speed_out[c, at, :] = speed[half, tile, cols(c)] * inverse
            return carry

        lax.fori_loop(0, PAIRS // 5, last, 0)

    out = []
    for c in range(3):
        inner = pl.ds(TOP + HALO, ROWS)
        out.append(
            pltpu.make_async_copy(place_out.at[c, inner, :], new_field.at[0, :, pl.ds(c * 128, 128)], sem_out.at[c])
        )
        out.append(
            pltpu.make_async_copy(speed_out.at[c, inner, :], new_moving.at[0, :, pl.ds(c * 128, 128)], sem_out.at[3 + c])
        )
    for copy in out:
        copy.start()
    for copy in out:
        copy.wait()


ANY = pl.BlockSpec(memory_space=pl.ANY)
IN_VMEM = pl.BlockSpec(memory_space=pltpu.VMEM)
DMA = pltpu.SemaphoreType.DMA
PLANE_3 = pltpu.VMEM((3, PLANE, 128), F32)
PLANE_1 = pltpu.VMEM((1, PLANE, 128), F32)
FULL = pltpu.VMEM((2, PAIR_ROWS, ROW), F32)
OPERAND = pltpu.VMEM((2, BAND_ROWS, ROW), BF16)
BANDS = [
    pltpu.VMEM((5 * ROW, 256), BF16),
    pltpu.VMEM((6 * ROW, 256), BF16),
    pltpu.VMEM((5 * ROW, 256), BF16),
]


def near(*arrays):
    return [pltpu.with_memory_space_constraint(a, pltpu.VMEM) for a in arrays]


def params(mib):
    return pltpu.CompilerParams(vmem_limit_bytes=mib * 2**20)


def per_device(
    displace, velocity, ext_force, inv_mass, thickness, stiff_bands, pair_points, pair_weights
):
    blocks = lax.axis_size("patch")
    points = pair_points.reshape(3, 1, SLOTS)
    weights = pair_weights.reshape(3, 1, SLOTS)
    near_pairs = [(i, i ^ 1) for i in range(blocks)]
    far_pairs = [(i, i + 1 if i % 2 else i - 1) for i in range(1, blocks - 1)]
    width = 3 * ROW + 2 * POINTS
    near_rows, far_rows = pl.pallas_call(
        bundle_kernel,
        out_shape=(pltpu.VMEM((HALO, width), F32), pltpu.VMEM((HALO, width), F32)),
        in_specs=[ANY] * 5,
        out_specs=[IN_VMEM] * 2,
        scratch_shapes=[DMA((10,))],
        compiler_params=params(2),
        name="bundle",
    )(*[pltpu.with_memory_space_constraint(a, pltpu.HBM) for a in [displace, velocity, ext_force, inv_mass, thickness]])
    far_rows = lax.ppermute(far_rows, "patch", far_pairs)
    near_rows = lax.ppermute(near_rows, "patch", near_pairs)

    field, operand, *bands = pl.pallas_call(
        load_kernel,
        out_shape=(PLANE_3, OPERAND, *BANDS),
        in_specs=[ANY] * 2,
        out_specs=[IN_VMEM] * 5,
        scratch_shapes=[DMA((3,)), DMA((20,))],
        compiler_params=params(2),
        name="load",
    )(displace, stiff_bands)

    slots = pltpu.VMEM((3, 1, SLOTS), F32)
    field, operand, moving, outer, mass, thick, force, compact, stiffest, *sends = pl.pallas_call(
        first_kernel,
        out_shape=(
            PLANE_3, OPERAND, PLANE_3, PLANE_3, PLANE_1, PLANE_1, FULL,
            pltpu.VMEM((PLANE, 128), F32), pltpu.VMEM((8, 128), F32), slots, slots, slots,
        ),
        in_specs=[IN_VMEM] * 8 + [ANY] * 4,
        out_specs=[IN_VMEM] * 12,
        scratch_shapes=[pltpu.VMEM((256, 256), BF16), DMA((3,)), DMA((3,)), DMA((1,)), DMA((1,))],
        input_output_aliases={0: 0, 1: 1},
        compiler_params=params(16),
        name="first_force",
    )(
        *near(field, operand, *bands, near_rows, far_rows, points),
        velocity, ext_force, inv_mass, thickness,
    )

    both = ("grp", "patch")
    mid_pairs = [(i, i) for i in range(blocks)]
    got = [
        lax.ppermute(
            send, both, [(g * blocks + i, (1 - g) * blocks + t) for g in range(2) for i, t in pairs]
        )
        for send, pairs in zip(sends, [far_pairs, mid_pairs, near_pairs])
    ]

    coupling, parcel = pl.pallas_call(
        couple_kernel,
        out_shape=(pltpu.VMEM((ROWS, 128), F32), pltpu.VMEM((2 * blocks, 1, 128), F32)),
        in_specs=[IN_VMEM] * 7,
        out_specs=[IN_VMEM] * 2,
        scratch_shapes=[pltpu.VMEM((128, 256), F32)],
        compiler_params=params(16),
        name="couple",
    )(*near(*got, points, weights, compact, stiffest))
    parcel = lax.all_to_all(parcel, both, 0, 0)

    new_field, new_moving = pl.pallas_call(
        step_kernel,
        out_shape=(
            jax.ShapeDtypeStruct((1, ROWS, ROW), F32),
            jax.ShapeDtypeStruct((1, ROWS, ROW), F32),
        ),
        in_specs=[IN_VMEM] * 11,
        out_specs=[ANY] * 2,
        scratch_shapes=[pltpu.VMEM((PLANE, 128), F32), FULL, FULL, FULL, pltpu.VMEM((2, PAIR_ROWS, 128), F32)]
        + [OPERAND, OPERAND, PLANE_3, PLANE_3, DMA((6,))],
        compiler_params=params(28),
        name="steps",
    )(*near(parcel, field, moving, outer, mass, thick, force, coupling, *bands))
    return new_field, new_moving


def solution(mesh):
    spec3 = P("grp", "patch", None)
    spec4 = P("grp", "patch", None, None)
    return jax.shard_map(
        per_device,
        mesh=mesh,
        in_specs=(spec3, spec3, spec3, spec3, spec3, P(), spec4, spec4),
        out_specs=(spec3, spec3),
        check_vma=False,
    )
```

```python
import jax
import jax.numpy as jnp
from jax import lax
from jax.experimental import pallas as pl
from jax.experimental.pallas import tpu as pltpu
from jax.sharding import PartitionSpec as P

POINTS = 128
REACH = 2
SUBSTEPS = 4
EDGE = 3
COURANT = 0.4
ROWS = 2048
ROW = 384
SLOTS = 1536
HALO = 8
RUN = 129
PAIRS = 65
PLANE = 2080
TOP = 8
PAIR_ROWS = PAIRS * 16
BAND_ROWS = (PAIRS + 2) * 16
CHUNK = 208
CHUNK_PAIRS = CHUNK // 16
F32 = jnp.float32
BF16 = jnp.bfloat16


def dot(a, b):
    return jnp.dot(a, b, preferred_element_type=F32)


def dot_nt(a, b):
    return lax.dot_general(a, b, (((1,), (1,)), ((), ())), preferred_element_type=F32)


def cols(c):
    return slice(c * 128, (c + 1) * 128)


def band_copies(stiff, wide_a, wide_b, wide_c, sem):
    copies = []
    for b in range(5):
        rows = pl.ds(b * ROW, ROW)
        next_rows = pl.ds((b + 1) * ROW, ROW)
        copies.append((stiff.at[b, :, pl.ds(0, 256)], wide_a.at[rows, :]))
        copies.append((stiff.at[b, :, pl.ds(256, 128)], wide_b.at[rows, pl.ds(0, 128)]))
        copies.append((stiff.at[b, :, pl.ds(0, 128)], wide_b.at[next_rows, pl.ds(128, 128)]))
        copies.append((stiff.at[b, :, pl.ds(128, 256)], wide_c.at[rows, :]))
    return [pltpu.make_async_copy(src, dst, sem.at[i]) for i, (src, dst) in enumerate(copies)]


def band_zeros(wide_b):
    wide_b[5 * ROW : 6 * ROW, 0:128] = jnp.zeros((ROW, 128), BF16)
    wide_b[0:ROW, 128:256] = jnp.zeros((ROW, 128), BF16)


def pair_products(parts, wide_a, wide_b, wide_c):
    part_a = dot(jnp.concatenate(parts[:5], axis=1), wide_a[...])
    part_b = dot(jnp.concatenate(parts, axis=1), wide_b[...])
    part_c = dot(jnp.concatenate(parts[1:], axis=1), wide_c[...])
    even = [part_a[:, 0:128], part_a[:, 128:256], part_b[:, 0:128]]
    odd = [part_b[:, 128:256], part_c[:, 0:128], part_c[:, 128:256]]
    return even, odd


def band_products(operand, start, count, wide_a, wide_b, wide_c):
    parts = [operand[i % 2, pl.ds(start + (i // 2) * 16, count), :] for i in range(6)]
    return pair_products(parts, wide_a, wide_b, wide_c)


def put_halo(plane, near, far, even, first, count):
    for c in range(count):
        column = slice(first + c * 128, first + c * 128 + 128)
        plane[c, TOP : TOP + HALO, :] = jnp.where(even, far[:, column], near[:, column])
        plane[c, TOP + HALO + ROWS : TOP + 2 * HALO + ROWS, :] = jnp.where(even, near[:, column], far[:, column])
        plane[c, 0:TOP, :] = jnp.zeros((TOP, 128), F32)
        plane[c, PLANE - 8 : PLANE, :] = jnp.zeros((8, 128), F32)


def plane_copies(array, plane, count, sem):
    return [
        pltpu.make_async_copy(
            array.at[0, :, pl.ds(c * 128, 128)], plane.at[c, pl.ds(TOP + HALO, ROWS), :], sem.at[c]
        )
        for c in range(count)
    ]


def spread(k):
    return pl.ds(TOP + k, 16, stride=RUN)


def bundle_kernel(displace, velocity, ext_force, inv_mass, thickness, near_rows, far_rows, sem):
    even = lax.axis_index("patch") % 2 == 0
    copies = []
    last = ROWS - HALO
    near_start = pl.multiple_of(jnp.where(even, last, 0), 8)
    far_start = pl.multiple_of(jnp.where(even, 0, last), 8)
    column = 0
    for array in [displace, velocity, ext_force, inv_mass, thickness]:
        width = array.shape[2]
        for rows, out in [(far_start, far_rows), (near_start, near_rows)]:
            copies.append(
                pltpu.make_async_copy(
                    array.at[0, pl.ds(rows, HALO), :], out.at[:, pl.ds(column, width)], sem.at[len(copies)]
                )
            )
        column += width
    for copy in copies:
        copy.start()
    for copy in copies:
        copy.wait()


def fill_operand(field, operand, step):
    for half in range(2):
        for c in range(3):
            operand[half, pl.ds(step * 16, 16), cols(c)] = field[c, spread(2 * step + half - 2), :].astype(BF16)


def load_kernel(displace, stiff, near_in, field, operand, wide_a, wide_b, wide_c, near_rows, sem_field, sem_band):
    field_in = plane_copies(displace, field, 3, sem_field)
    bands_in = band_copies(stiff, wide_a, wide_b, wide_c, sem_band)
    for copy in field_in + bands_in:
        copy.start()
    for c in range(3):
        field[c, 0 : TOP + HALO, :] = jnp.zeros((TOP + HALO, 128), F32)
        field[c, TOP + HALO + ROWS : PLANE, :] = jnp.zeros((PLANE - TOP - HALO - ROWS, 128), F32)
    band_zeros(wide_b)
    for copy in field_in:
        copy.wait()

    def some(i, carry):
        for j in range(4):
            fill_operand(field, operand, pl.multiple_of(i * 4, 4) + j + 3)
        return carry

    for step in range(3):
        fill_operand(field, operand, step)
    lax.fori_loop(0, (PAIRS - 1) // 4, some, 0)
    for copy in bands_in:
        copy.wait()


def slot_place(entry):
    row = (entry * 21846) >> 16
    return row >> 7, row & 127, entry - 3 * row


def compact_rows(step, field, moving, thick, compact, force):
    lane = lax.broadcasted_iota(jnp.int32, (16, 128), 1)
    for half in range(2):
        at = spread(2 * step + half)
        half_thick = 0.5 * thick[0, at, :]
        parts = [field[c, at, :] + 0.5 * moving[c, at, :] + half_thick * force[half][c] for c in range(3)]
        compact[at, :] = jnp.where(
            lane < 3,
            parts[0],
            jnp.where(lane < 6, pltpu.roll(parts[1], 3, 1), pltpu.roll(parts[2], 6, 1)),
        )


def some_rows(results, i):
    return [[part[i * 16 : i * 16 + 16, :] for part in half] for half in results]


def force_kernel(
    field, operand, wide_a, wide_b, wide_c, velocity, ext_force, inv_mass, thickness,
    moving, outer, mass, thick, force, compact, stiffest,
    sem_moving, sem_outer, sem_mass, sem_thick,
):
    thick_in = plane_copies(thickness, thick, 1, sem_thick)
    moving_in = plane_copies(velocity, moving, 3, sem_moving)
    mass_in = plane_copies(inv_mass, mass, 1, sem_mass)
    outer_in = plane_copies(ext_force, outer, 3, sem_outer)
    for copy in thick_in + moving_in + mass_in + outer_in:
        copy.start()

    def make_compact(start, results):
        for i in range(CHUNK_PAIRS):
            compact_rows(start // 16 + i, field, moving, thick, compact, some_rows(results, i))

    before = None
    for start in range(0, PAIR_ROWS, CHUNK):
        results = band_products(operand, start, CHUNK, wide_a, wide_b, wide_c)
        for half in range(2):
            for c in range(3):
                force[half, start : start + CHUNK, cols(c)] = results[half][c]
        if before is None:
            for copy in thick_in + moving_in:
                copy.wait()
        else:
            make_compact(*before)
        before = (start, results)
    for copy in mass_in:
        copy.wait()
    product = jnp.zeros((8, 128), F32)
    for i in range(8):
        rows = slice(TOP + HALO + i * 256, TOP + HALO + i * 256 + 256)
        product = jnp.maximum(
            product, jnp.max((mass[0, rows, :] * thick[0, rows, :]).reshape(32, 8, 128), axis=0)
        )
    most = jnp.max(jnp.max(product, axis=0, keepdims=True), axis=1, keepdims=True)
    stiffest[...] = jnp.broadcast_to(most, (8, 128))
    make_compact(*before)
    for copy in outer_in:
        copy.wait()


def pick_slots(entry, table, send):
    place = lax.broadcasted_iota(jnp.int32, (128, SLOTS), 0)
    group_of, low, point = slot_place(entry)
    chosen = jnp.where(place == low, 1.0, 0.0).astype(BF16)
    picked = dot(table[...], jnp.concatenate([chosen, chosen], axis=0))
    total = jnp.zeros((16, SLOTS), F32)
    for group in range(16):
        total = total + jnp.where(group_of == group, picked[group * 16 : group * 16 + 16, :], 0.0)
    for c in range(3):
        send[c] = jnp.where(
            point == 0,
            total[3 * c : 3 * c + 1, :],
            jnp.where(point == 1, total[3 * c + 1 : 3 * c + 2, :], total[3 * c + 2 : 3 * c + 3, :]),
        )


def near_offset():
    return jnp.where(lax.axis_index("patch") % 2 == 0, 2, 0)


FAR_ROWS = 5
LOW_PAIRS = 5
HIGH_PAIR = 59


def ends_kernel(
    wide_a, wide_b, wide_c, near_rows, far_rows, points,
    field_in, operand_in, moving_in, outer_in, mass_in, thick_in, force_in, compact_in,
    field, operand, moving, outer, mass, thick, force, compact, table, send_far,
):
    even = lax.axis_index("patch") % 2 == 0
    put_halo(field, near_rows, far_rows, even, 0, 3)
    put_halo(moving, near_rows, far_rows, even, 384, 3)
    put_halo(outer, near_rows, far_rows, even, 768, 3)
    put_halo(mass, near_rows, far_rows, even, 1152, 1)
    put_halo(thick, near_rows, far_rows, even, 1280, 1)
    for step in list(range(6)) + list(range(60, 67)):
        fill_operand(field, operand, step)
    low = LOW_PAIRS * 16
    high = (PAIRS - HIGH_PAIR) * 16
    parts = [
        jnp.concatenate(
            [
                operand[i % 2, (i // 2) * 16 : (i // 2) * 16 + low, :],
                operand[i % 2, (HIGH_PAIR + i // 2) * 16 : (HIGH_PAIR + i // 2) * 16 + high, :],
            ],
            axis=0,
        )
        for i in range(6)
    ]
    results = pair_products(parts, wide_a, wide_b, wide_c)
    for half in range(2):
        for c in range(3):
            force[half, 0:low, cols(c)] = results[half][c][:low]
            force[half, HIGH_PAIR * 16 : PAIR_ROWS, cols(c)] = results[half][c][low:]
    for i, step in enumerate(list(range(LOW_PAIRS)) + list(range(HIGH_PAIR, PAIRS))):
        compact_rows(step, field, moving, thick, compact, some_rows(results, i))
    for group in range(16):
        start = TOP + HALO + group * 128
        turned = compact[start : start + 128, :].T[0:16, :]
        upper = turned.astype(BF16)
        table[group * 16 : group * 16 + 16, 0:128] = upper
        table[group * 16 : group * 16 + 16, 128:256] = (turned - upper.astype(F32)).astype(BF16)
    pick_slots(points[2 - near_offset()], table, send_far)
    for c in range(3, FAR_ROWS):
        send_far[c] = jnp.zeros((1, SLOTS), F32)


def pick_kernel(table, points, stiffest, send_mid, send_near):
    send_mid[3] = jnp.concatenate([stiffest[0:1, :]] * (SLOTS // 128), axis=1)
    pick_slots(points[1], table, send_mid)
    pick_slots(points[near_offset()], table, send_near)


def sum_slots(j, got, points, weights):
    place = lax.broadcasted_iota(jnp.int32, (128, SLOTS), 0)
    line = lax.broadcasted_iota(jnp.int32, (16, SLOTS), 0)
    group_of, low, point = slot_place(points[j])
    neighbour = lax.axis_index("patch") + (j - 1)
    present = jnp.where((neighbour >= 0) & (neighbour < lax.axis_size("patch")), 1.0, 0.0)
    weight = weights[j] * present
    spread_out = jnp.zeros((16, SLOTS), F32)
    for c in range(4):
        value = weight * got[c] if c < 3 else weight
        spread_out = jnp.where(line == 3 * c + point, value, spread_out)
    high = spread_out.astype(BF16)
    rest = (spread_out - high.astype(F32)).astype(BF16)
    zero = jnp.zeros((16, SLOTS), BF16)
    right = jnp.concatenate(
        [jnp.where(group_of == group, high, zero) for group in range(16)]
        + [jnp.where(group_of == group, rest, zero) for group in range(16)],
        axis=0,
    )
    chosen = jnp.where(place == low, 1.0, 0.0).astype(BF16)
    part = dot_nt(chosen, right)
    return part[:, 0:256] + part[:, 256:512]


def half_couple_kernel(got_mid, got_near, points, weights, stiffest, partial, most):
    partial[...] = sum_slots(1, got_mid, points, weights) + sum_slots(near_offset(), got_near, points, weights)
    most[...] = jnp.maximum(stiffest[...], jnp.broadcast_to(got_mid[3][:, 0:128], (8, 128)))


def couple_kernel(got_far, points, weights, partial, most, compact, coupling, parcel, total):
    block = lax.axis_index("patch")
    blocks = lax.axis_size("patch")
    total[...] = partial[...] + sum_slots(2 - near_offset(), got_far, points, weights)
    lane = lax.broadcasted_iota(jnp.int32, (128, 128), 1)
    edges = []
    for group in range(16):
        half = total[:, (group // 8) * 128 : (group // 8) * 128 + 128]
        shift = (group % 8) * 16
        block_sum = pltpu.roll(half, 128 - shift, 1) if shift else half
        weight_sum = jnp.where(
            lane < 3,
            pltpu.roll(block_sum, 119, 1),
            jnp.where(lane < 6, pltpu.roll(block_sum, 122, 1), pltpu.roll(block_sum, 125, 1)),
        )
        start = TOP + HALO + group * 128
        here = block_sum - compact[start : start + 128, :] * weight_sum
        here = jnp.where(lane < 9, here, 0.0)
        coupling[start : start + 128, :] = here
        if group == 0:
            edges.append(here[0:8, :])
        if group == 15:
            edges.append(here[120:128, :])
    lane_row = lax.broadcasted_iota(jnp.int32, (1, 128), 1)
    flat = []
    for edge in edges:
        line_up = edge[0:1, :]
        for row in range(1, 8):
            line_up = line_up + pltpu.roll(edge, 16 * row, 1)[row : row + 1, :]
        flat.append(jnp.where(lane_row == 15, most[0:1, :], line_up))
    parcel[...] = jnp.broadcast_to(flat[0][None], (blocks, 1, 128))
    parcel[jnp.minimum(block + 1, blocks - 1)] = flat[1]


def step_kernel(
    parcel, field, moving, outer, mass, thick, force, coupling_in, wide_a, wide_b, wide_c,
    new_field, new_moving, couple,
    state, speed, push, drag, operand_a, operand_b, place_out, speed_out, sem_out,
):
    block = lax.axis_index("patch")
    blocks = lax.axis_size("patch")
    fine = lax.axis_index("grp") == 1
    lane_row = lax.broadcasted_iota(jnp.int32, (1, 128), 1)
    sublane = lax.broadcasted_iota(jnp.int32, (8, 128), 0)
    most = jnp.max(parcel[...].reshape(blocks, 128), axis=0, keepdims=True)
    most = jnp.max(jnp.where(lane_row == 15, most, 0.0), axis=1, keepdims=True)
    limit = jnp.broadcast_to(most, (16, 128))
    base_step = COURANT * (1.0 / jnp.sqrt(limit))
    size = jnp.where(fine, base_step, SUBSTEPS * base_step)
    square = size * size
    inverse = 1.0 / size
    for start, there, exists in [
        (TOP, jnp.maximum(block - 1, 0), block > 0),
        (TOP + HALO + ROWS, jnp.minimum(block + 1, blocks - 1), block < blocks - 1),
    ]:
        line_up = jnp.broadcast_to(parcel[there], (8, 128))
        edge = line_up
        for row in range(1, 8):
            edge = jnp.where(sublane == row, pltpu.roll(line_up, 128 - 16 * row, 1), edge)
        edge = jnp.where(lax.broadcasted_iota(jnp.int32, (8, 128), 1) < 9, edge, 0.0)
        couple[start : start + 8, :] = jnp.where(exists, edge, 0.0)
    couple[0:TOP, :] = jnp.zeros((TOP, 128), F32)
    couple[PLANE - 8 : PLANE, :] = jnp.zeros((8, 128), F32)
    lane = lax.broadcasted_iota(jnp.int32, (16, 128), 1)

    def first_update(step, keep):
        for half in range(2):
            at = spread(2 * step + half)
            tile = pl.ds(step * 16, 16) if isinstance(step, int) else pl.ds(pl.multiple_of(step * 16, 16), 16)
            scaled = square * mass[0, at, :]
            pull = scaled * thick[0, at, :]
            both = couple[at, :]
            if keep:
                drag[half, tile, :] = pull
            for c in range(3):
                here = jnp.where(lane < 3, pltpu.roll(both, 128 - 3 * c, 1) if c else both, 0.0)
                drive = scaled * (outer[c, at, :] + here)
                new_speed = size * moving[c, at, :] + (drive - pull * force[half, tile, cols(c)])
                place = field[c, at, :] + new_speed
                if keep:
                    push[half, tile, cols(c)] = drive
                    speed[half, tile, cols(c)] = new_speed
                    state[half, tile, cols(c)] = place
                    operand_a[half, step * 16 + 16 : step * 16 + 32, cols(c)] = place.astype(BF16)
                else:
                    place_out[c, at, :] = place
                    speed_out[c, at, :] = new_speed * inverse

    @pl.when(jnp.logical_not(fine))
    def _():
        def some(turn, carry):
            for i in range(5):
                first_update(turn * 5 + i, False)
            return carry

        lax.fori_loop(0, PAIRS // 5, some, 0)

    def low_ends(operand):
        for c in range(3):
            operand[0, 0:16, cols(c)] = pltpu.roll(state[1, 63 * 16 : 64 * 16, cols(c)], 1, 0).astype(BF16)
            operand[1, 0:16, cols(c)] = pltpu.roll(state[0, 64 * 16 : 65 * 16, cols(c)], 1, 0).astype(BF16)

    def high_ends(operand):
        for c in range(3):
            operand[0, 66 * 16 : 67 * 16, cols(c)] = pltpu.roll(state[1, 0:16, cols(c)], 15, 0).astype(BF16)
            operand[1, 66 * 16 : 67 * 16, cols(c)] = pltpu.roll(state[0, 16:32, cols(c)], 15, 0).astype(BF16)

    def update(chunk, results, following):
        start = chunk * CHUNK
        rows = slice(start, start + CHUNK)
        for half in range(2):
            pull = drag[half, rows, :]
            for c in range(3):
                new_speed = speed[half, rows, cols(c)] + (push[half, rows, cols(c)] - pull * results[half][c])
                place = state[half, rows, cols(c)] + new_speed
                if following is not None:
                    speed[half, rows, cols(c)] = new_speed
                    state[half, rows, cols(c)] = place
                    following[half, start + 16 : start + 16 + CHUNK, cols(c)] = place.astype(BF16)
                else:
                    for i in range(CHUNK_PAIRS):
                        at = spread(2 * (start // 16 + i) + half)
                        place_out[c, at, :] = place[i * 16 : i * 16 + 16, :]
                        speed_out[c, at, :] = new_speed[i * 16 : i * 16 + 16, :] * inverse
        if following is not None and chunk == 0:
            high_ends(following)
        if following is not None and chunk == PAIR_ROWS // CHUNK - 1:
            low_ends(following)

    @pl.when(fine)
    def _():
        for step in [63, 64] + list(range(CHUNK_PAIRS + 1)):
            first_update(step, True)
        low_ends(operand_a)
        high_ends(operand_a)
        before = None
        for operand, following, order in [
            (operand_a, operand_b, [0, 1, 2, 3, 4]),
            (operand_b, operand_a, [1, 2, 3, 4, 0]),
            (operand_a, None, [2, 3, 4, 0, 1]),
        ]:
            for chunk in order:
                results = band_products(operand, chunk * CHUNK, CHUNK, wide_a, wide_b, wide_c)
                if operand is operand_a and following is operand_b:
                    first = (chunk + 1) * CHUNK_PAIRS + 1
                    for step in range(first, min(first + CHUNK_PAIRS, 63)):
                        first_update(step, True)
                if before is not None:
                    update(*before)
                before = (chunk, results, following)
        update(*before)

    out = []
    for c in range(3):
        inner = pl.ds(TOP + HALO, ROWS)
        out.append(
            pltpu.make_async_copy(place_out.at[c, inner, :], new_field.at[0, :, pl.ds(c * 128, 128)], sem_out.at[c])
        )
        out.append(
            pltpu.make_async_copy(speed_out.at[c, inner, :], new_moving.at[0, :, pl.ds(c * 128, 128)], sem_out.at[3 + c])
        )
    for copy in out:
        copy.start()
    for copy in out:
        copy.wait()


ANY = pl.BlockSpec(memory_space=pl.ANY)
IN_VMEM = pl.BlockSpec(memory_space=pltpu.VMEM)
DMA = pltpu.SemaphoreType.DMA
PLANE_3 = pltpu.VMEM((3, PLANE, 128), F32)
PLANE_1 = pltpu.VMEM((1, PLANE, 128), F32)
FULL = pltpu.VMEM((2, PAIR_ROWS, ROW), F32)
OPERAND = pltpu.VMEM((2, BAND_ROWS, ROW), BF16)
BANDS = [
    pltpu.VMEM((5 * ROW, 256), BF16),
    pltpu.VMEM((6 * ROW, 256), BF16),
    pltpu.VMEM((5 * ROW, 256), BF16),
]


def near(*arrays):
    return [pltpu.with_memory_space_constraint(a, pltpu.VMEM) for a in arrays]


def params(mib):
    return pltpu.CompilerParams(vmem_limit_bytes=mib * 2**20)


def per_device(
    displace, velocity, ext_force, inv_mass, thickness, stiff_bands, pair_points, pair_weights
):
    blocks = lax.axis_size("patch")
    points = pair_points.reshape(3, 1, SLOTS)
    weights = pair_weights.reshape(3, 1, SLOTS)
    near_pairs = [(i, i ^ 1) for i in range(blocks)]
    far_pairs = [(i, i + 1 if i % 2 else i - 1) for i in range(1, blocks - 1)]
    width = 3 * ROW + 2 * POINTS
    near_rows, far_rows = pl.pallas_call(
        bundle_kernel,
        out_shape=(pltpu.VMEM((HALO, width), F32), pltpu.VMEM((HALO, width), F32)),
        in_specs=[ANY] * 5,
        out_specs=[IN_VMEM] * 2,
        scratch_shapes=[DMA((10,))],
        compiler_params=params(2),
        name="bundle",
    )(*[pltpu.with_memory_space_constraint(a, pltpu.HBM) for a in [displace, velocity, ext_force, inv_mass, thickness]])
    far_rows = lax.ppermute(far_rows, "patch", far_pairs)

    field, operand, *bands, near_rows = pl.pallas_call(
        load_kernel,
        out_shape=(PLANE_3, OPERAND, *BANDS, pltpu.VMEM((HALO, width), F32)),
        in_specs=[ANY] * 2 + [IN_VMEM],
        out_specs=[IN_VMEM] * 6,
        input_output_aliases={2: 5},
        scratch_shapes=[DMA((3,)), DMA((20,))],
        compiler_params=params(2),
        name="load",
    )(displace, stiff_bands, *near(near_rows))
    near_rows = lax.ppermute(near_rows, "patch", near_pairs)

    plane = pltpu.VMEM((PLANE, 128), F32)
    tile = pltpu.VMEM((8, 128), F32)
    moving, outer, mass, thick, force, compact, stiffest = pl.pallas_call(
        force_kernel,
        out_shape=(PLANE_3, PLANE_3, PLANE_1, PLANE_1, FULL, plane, tile),
        in_specs=[IN_VMEM] * 5 + [ANY] * 4,
        out_specs=[IN_VMEM] * 7,
        scratch_shapes=[DMA((3,)), DMA((3,)), DMA((1,)), DMA((1,))],
        compiler_params=params(12),
        name="force",
    )(*near(field, operand, *bands), velocity, ext_force, inv_mass, thickness)

    slots = pltpu.VMEM((3, 1, SLOTS), F32)
    table = pltpu.VMEM((256, 256), BF16)
    field, operand, moving, outer, mass, thick, force, compact, table, send_far = pl.pallas_call(
        ends_kernel,
        out_shape=(PLANE_3, OPERAND, PLANE_3, PLANE_3, PLANE_1, PLANE_1, FULL, plane, table, pltpu.VMEM((FAR_ROWS, 1, SLOTS), F32)),
        in_specs=[IN_VMEM] * 14,
        out_specs=[IN_VMEM] * 10,
        input_output_aliases={i + 6: i for i in range(8)},
        compiler_params=params(12),
        name="ends",
    )(*near(*bands, near_rows, far_rows, points, field, operand, moving, outer, mass, thick, force, compact))

    both = ("grp", "patch")
    mid_pairs = [(i, i) for i in range(blocks)]

    def across(send, pairs):
        return lax.ppermute(
            send, both, [(g * blocks + i, (1 - g) * blocks + t) for g in range(2) for i, t in pairs]
        )

    got_far = across(send_far, far_pairs)
    send_mid, send_near = pl.pallas_call(
        pick_kernel,
        out_shape=(pltpu.VMEM((4, 1, SLOTS), F32), slots),
        in_specs=[IN_VMEM] * 3,
        out_specs=[IN_VMEM] * 2,
        compiler_params=params(12),
        cost_estimate=pl.CostEstimate(flops=1, transcendentals=0, bytes_accessed=1),
        name="pick",
    )(*near(table, points, stiffest))
    got_mid = across(send_mid, mid_pairs)
    got_near = across(send_near, near_pairs)
    partial, most = pl.pallas_call(
        half_couple_kernel,
        out_shape=(pltpu.VMEM((128, 256), F32), tile),
        in_specs=[IN_VMEM] * 5,
        out_specs=[IN_VMEM] * 2,
        compiler_params=params(12),
        cost_estimate=pl.CostEstimate(flops=1, transcendentals=0, bytes_accessed=1),
        name="half_couple",
    )(*near(got_mid, got_near, points, weights, stiffest))
    coupling, parcel = pl.pallas_call(
        couple_kernel,
        out_shape=(plane, pltpu.VMEM((blocks, 1, 128), F32)),
        in_specs=[IN_VMEM] * 6,
        out_specs=[IN_VMEM] * 2,
        scratch_shapes=[pltpu.VMEM((128, 256), F32)],
        compiler_params=params(12),
        name="couple",
    )(*near(got_far, points, weights, partial, most, compact))
    parcel = lax.all_to_all(parcel, "patch", 0, 0)

    new_field, new_moving, unused = pl.pallas_call(
        step_kernel,
        out_shape=(
            jax.ShapeDtypeStruct((1, ROWS, ROW), F32),
            jax.ShapeDtypeStruct((1, ROWS, ROW), F32),
            pltpu.VMEM((PLANE, 128), F32),
        ),
        in_specs=[IN_VMEM] * 11,
        out_specs=[ANY] * 2 + [IN_VMEM],
        input_output_aliases={7: 2},
        scratch_shapes=[FULL, FULL, FULL, pltpu.VMEM((2, PAIR_ROWS, 128), F32)]
        + [OPERAND, OPERAND, PLANE_3, PLANE_3, DMA((6,))],
        compiler_params=params(28),
        name="steps",
    )(*near(parcel, field, moving, outer, mass, thick, force, coupling, *bands))
    return new_field, new_moving


def solution(mesh):
    spec3 = P("grp", "patch", None)
    spec4 = P("grp", "patch", None, None)
    return jax.shard_map(
        per_device,
        mesh=mesh,
        in_specs=(spec3, spec3, spec3, spec3, spec3, P(), spec4, spec4),
        out_specs=(spec3, spec3),
        check_vma=False,
    )
```

```python
import jax
import jax.numpy as jnp
from jax import lax
from jax.experimental import pallas as pl
from jax.experimental.pallas import tpu as pltpu
from jax.sharding import PartitionSpec as P

POINTS = 128
REACH = 2
SUBSTEPS = 4
EDGE = 3
COURANT = 0.4
ROWS = 2048
ROW = 384
SLOTS = 1536
HALO = 8
RUN = 129
PAIRS = 65
PLANE = 2080
TOP = 8
PAIR_ROWS = PAIRS * 16
BAND_ROWS = (PAIRS + 2) * 16
CHUNK = 208
CHUNK_PAIRS = CHUNK // 16
F32 = jnp.float32
BF16 = jnp.bfloat16


def dot(a, b):
    return jnp.dot(a, b, preferred_element_type=F32)


def dot_nt(a, b):
    return lax.dot_general(a, b, (((1,), (1,)), ((), ())), preferred_element_type=F32)


def cols(c):
    return slice(c * 128, (c + 1) * 128)


def band_copies(stiff, wide_a, wide_b, wide_c, sem):
    copies = []
    for b in range(5):
        rows = pl.ds(b * ROW, ROW)
        next_rows = pl.ds((b + 1) * ROW, ROW)
        copies.append((stiff.at[b, :, pl.ds(0, 256)], wide_a.at[rows, :]))
        copies.append((stiff.at[b, :, pl.ds(256, 128)], wide_b.at[rows, pl.ds(0, 128)]))
        copies.append((stiff.at[b, :, pl.ds(0, 128)], wide_b.at[next_rows, pl.ds(128, 128)]))
        copies.append((stiff.at[b, :, pl.ds(128, 256)], wide_c.at[rows, :]))
    return [pltpu.make_async_copy(src, dst, sem.at[i]) for i, (src, dst) in enumerate(copies)]


def band_zeros(wide_b):
    wide_b[5 * ROW : 6 * ROW, 0:128] = jnp.zeros((ROW, 128), BF16)
    wide_b[0:ROW, 128:256] = jnp.zeros((ROW, 128), BF16)


def pair_products(parts, wide_a, wide_b, wide_c):
    part_a = dot(jnp.concatenate(parts[:5], axis=1), wide_a[...])
    part_b = dot(jnp.concatenate(parts, axis=1), wide_b[...])
    part_c = dot(jnp.concatenate(parts[1:], axis=1), wide_c[...])
    even = [part_a[:, 0:128], part_a[:, 128:256], part_b[:, 0:128]]
    odd = [part_b[:, 128:256], part_c[:, 0:128], part_c[:, 128:256]]
    return even, odd


def band_products(operand, start, count, wide_a, wide_b, wide_c):
    parts = [operand[i % 2, pl.ds(start + (i // 2) * 16, count), :] for i in range(6)]
    return pair_products(parts, wide_a, wide_b, wide_c)


def put_halo(plane, near, far, even, first, count):
    for c in range(count):
        column = slice(first + c * 128, first + c * 128 + 128)
        plane[c, TOP : TOP + HALO, :] = jnp.where(even, far[:, column], near[:, column])
        plane[c, TOP + HALO + ROWS : TOP + 2 * HALO + ROWS, :] = jnp.where(even, near[:, column], far[:, column])
        plane[c, 0:TOP, :] = jnp.zeros((TOP, 128), F32)
        plane[c, PLANE - 8 : PLANE, :] = jnp.zeros((8, 128), F32)


def plane_copies(array, plane, count, sem):
    return [
        pltpu.make_async_copy(
            array.at[0, :, pl.ds(c * 128, 128)], plane.at[c, pl.ds(TOP + HALO, ROWS), :], sem.at[c]
        )
        for c in range(count)
    ]


def spread(k):
    return pl.ds(TOP + k, 16, stride=RUN)


def bundle_kernel(displace, velocity, ext_force, inv_mass, thickness, near_rows, far_rows, sem):
    even = lax.axis_index("patch") % 2 == 0
    copies = []
    last = ROWS - HALO
    near_start = pl.multiple_of(jnp.where(even, last, 0), 8)
    far_start = pl.multiple_of(jnp.where(even, 0, last), 8)
    column = 0
    for array in [displace, velocity, ext_force, inv_mass, thickness]:
        width = array.shape[2]
        for rows, out in [(far_start, far_rows), (near_start, near_rows)]:
            copies.append(
                pltpu.make_async_copy(
                    array.at[0, pl.ds(rows, HALO), :], out.at[:, pl.ds(column, width)], sem.at[len(copies)]
                )
            )
        column += width
    for copy in copies:
        copy.start()
    for copy in copies:
        copy.wait()


def fill_operand(field, operand, step):
    for half in range(2):
        for c in range(3):
            operand[half, pl.ds(step * 16, 16), cols(c)] = field[c, spread(2 * step + half - 2), :].astype(BF16)


def load_kernel(displace, stiff, near_in, field, operand, wide_a, wide_b, wide_c, near_rows, sem_field, sem_band):
    field_in = plane_copies(displace, field, 3, sem_field)
    bands_in = band_copies(stiff, wide_a, wide_b, wide_c, sem_band)
    for copy in field_in + bands_in:
        copy.start()
    for c in range(3):
        field[c, 0 : TOP + HALO, :] = jnp.zeros((TOP + HALO, 128), F32)
        field[c, TOP + HALO + ROWS : PLANE, :] = jnp.zeros((PLANE - TOP - HALO - ROWS, 128), F32)
    band_zeros(wide_b)
    for copy in field_in:
        copy.wait()

    def some(i, carry):
        for j in range(4):
            fill_operand(field, operand, pl.multiple_of(i * 4, 4) + j + 3)
        return carry

    for step in range(3):
        fill_operand(field, operand, step)
    lax.fori_loop(0, (PAIRS - 1) // 4, some, 0)
    for copy in bands_in:
        copy.wait()


def slot_place(entry):
    row = (entry * 21846) >> 16
    return row >> 7, row & 127, entry - 3 * row


def compact_rows(step, field, moving, thick, compact, force):
    lane = lax.broadcasted_iota(jnp.int32, (16, 128), 1)
    for half in range(2):
        at = spread(2 * step + half)
        half_thick = 0.5 * thick[0, at, :]
        parts = [field[c, at, :] + 0.5 * moving[c, at, :] + half_thick * force[half][c] for c in range(3)]
        compact[at, :] = jnp.where(
            lane < 3,
            parts[0],
            jnp.where(lane < 6, pltpu.roll(parts[1], 3, 1), pltpu.roll(parts[2], 6, 1)),
        )


def some_rows(results, i):
    return [[part[i * 16 : i * 16 + 16, :] for part in half] for half in results]


def force_kernel(
    field, operand, wide_a, wide_b, wide_c, velocity, ext_force, inv_mass, thickness,
    moving, outer, mass, thick, force, compact, stiffest,
    sem_moving, sem_outer, sem_mass, sem_thick,
):
    thick_in = plane_copies(thickness, thick, 1, sem_thick)
    moving_in = plane_copies(velocity, moving, 3, sem_moving)
    mass_in = plane_copies(inv_mass, mass, 1, sem_mass)
    outer_in = plane_copies(ext_force, outer, 3, sem_outer)
    for copy in thick_in + moving_in + mass_in + outer_in:
        copy.start()

    def make_compact(start, results):
        for i in range(CHUNK_PAIRS):
            compact_rows(start // 16 + i, field, moving, thick, compact, some_rows(results, i))

    before = None
    for start in range(0, PAIR_ROWS, CHUNK):
        results = band_products(operand, start, CHUNK, wide_a, wide_b, wide_c)
        for half in range(2):
            for c in range(3):
                force[half, start : start + CHUNK, cols(c)] = results[half][c]
        if before is None:
            for copy in thick_in + moving_in:
                copy.wait()
        else:
            make_compact(*before)
        before = (start, results)
    for copy in mass_in:
        copy.wait()
    product = jnp.zeros((8, 128), F32)
    for i in range(8):
        rows = slice(TOP + HALO + i * 256, TOP + HALO + i * 256 + 256)
        product = jnp.maximum(
            product, jnp.max((mass[0, rows, :] * thick[0, rows, :]).reshape(32, 8, 128), axis=0)
        )
    most = jnp.max(jnp.max(product, axis=0, keepdims=True), axis=1, keepdims=True)
    stiffest[...] = jnp.broadcast_to(most, (8, 128))
    make_compact(*before)
    for copy in outer_in:
        copy.wait()


def pick_slots(entry, table, send):
    place = lax.broadcasted_iota(jnp.int32, (128, SLOTS), 0)
    group_of, low, point = slot_place(entry)
    chosen = jnp.where(place == low, 1.0, 0.0).astype(BF16)
    picked = dot(table[...], jnp.concatenate([chosen, chosen], axis=0))
    total = jnp.zeros((16, SLOTS), F32)
    for group in range(16):
        total = total + jnp.where(group_of == group, picked[group * 16 : group * 16 + 16, :], 0.0)
    for c in range(3):
        send[c] = jnp.where(
            point == 0,
            total[3 * c : 3 * c + 1, :],
            jnp.where(point == 1, total[3 * c + 1 : 3 * c + 2, :], total[3 * c + 2 : 3 * c + 3, :]),
        )


def near_offset():
    return jnp.where(lax.axis_index("patch") % 2 == 0, 2, 0)


FAR_ROWS = 5
LOW_PAIRS = 5
HIGH_PAIR = 59


def ends_kernel(
    wide_a, wide_b, wide_c, near_rows, far_rows, points,
    field_in, operand_in, moving_in, outer_in, mass_in, thick_in, force_in, compact_in,
    field, operand, moving, outer, mass, thick, force, compact, table, send_far,
):
    even = lax.axis_index("patch") % 2 == 0
    put_halo(field, near_rows, far_rows, even, 0, 3)
    put_halo(moving, near_rows, far_rows, even, 384, 3)
    put_halo(outer, near_rows, far_rows, even, 768, 3)
    put_halo(mass, near_rows, far_rows, even, 1152, 1)
    put_halo(thick, near_rows, far_rows, even, 1280, 1)
    for step in list(range(6)) + list(range(60, 67)):
        fill_operand(field, operand, step)
    low = LOW_PAIRS * 16
    high = (PAIRS - HIGH_PAIR) * 16
    parts = [
        jnp.concatenate(
            [
                operand[i % 2, (i // 2) * 16 : (i // 2) * 16 + low, :],
                operand[i % 2, (HIGH_PAIR + i // 2) * 16 : (HIGH_PAIR + i // 2) * 16 + high, :],
            ],
            axis=0,
        )
        for i in range(6)
    ]
    results = pair_products(parts, wide_a, wide_b, wide_c)
    for half in range(2):
        for c in range(3):
            force[half, 0:low, cols(c)] = results[half][c][:low]
            force[half, HIGH_PAIR * 16 : PAIR_ROWS, cols(c)] = results[half][c][low:]
    for i, step in enumerate(list(range(LOW_PAIRS)) + list(range(HIGH_PAIR, PAIRS))):
        compact_rows(step, field, moving, thick, compact, some_rows(results, i))
    for group in range(16):
        start = TOP + HALO + group * 128
        turned = compact[start : start + 128, :].T[0:16, :]
        upper = turned.astype(BF16)
        table[group * 16 : group * 16 + 16, 0:128] = upper
        table[group * 16 : group * 16 + 16, 128:256] = (turned - upper.astype(F32)).astype(BF16)
    pick_slots(points[2 - near_offset()], table, send_far)
    for c in range(3, FAR_ROWS):
        send_far[c] = jnp.zeros((1, SLOTS), F32)


def pick_kernel(table, points, stiffest, send_mid, send_near):
    send_mid[3] = jnp.concatenate([stiffest[0:1, :]] * (SLOTS // 128), axis=1)
    pick_slots(points[1], table, send_mid)
    pick_slots(points[near_offset()], table, send_near)


def slot_weight(j, weights):
    neighbour = lax.axis_index("patch") + (j - 1)
    present = jnp.where((neighbour >= 0) & (neighbour < lax.axis_size("patch")), 1.0, 0.0)
    return weights[j] * present


def own_kernel(points, weights, compact, own, total):
    place = lax.broadcasted_iota(jnp.int32, (128, SLOTS), 0)
    line = lax.broadcasted_iota(jnp.int32, (16, SLOTS), 0)
    summed = None
    for j in range(3):
        group_of, low, point = slot_place(points[j])
        weight = slot_weight(j, weights)
        upper = weight.astype(BF16).astype(F32)
        both = jnp.where(line == point, upper, jnp.where(line == point + 8, weight - upper, 0.0)).astype(BF16)
        zero = jnp.zeros((16, SLOTS), BF16)
        right = jnp.concatenate([jnp.where(group_of == group, both, zero) for group in range(16)], axis=0)
        part = dot_nt(jnp.where(place == low, 1.0, 0.0).astype(BF16), right)
        summed = part if summed is None else summed + part
    total[...] = summed
    lane = lax.broadcasted_iota(jnp.int32, (128, 128), 1)
    for group in range(16):
        half = total[:, (group // 8) * 128 : (group // 8) * 128 + 128]
        half = half + pltpu.roll(half, 120, 1)
        shift = (group % 8) * 16
        weight_sum = jnp.where(
            lane < 3,
            pltpu.roll(half, 128 - shift, 1) if shift else half,
            jnp.where(
                lane < 6,
                pltpu.roll(half, (131 - shift) % 128, 1),
                pltpu.roll(half, (134 - shift) % 128, 1),
            ),
        )
        start = TOP + HALO + group * 128
        own[group * 128 : group * 128 + 128, :] = jnp.where(
            lane < 9, compact[start : start + 128, :] * weight_sum, 0.0
        )


def sum_slots(j, got, points, weights):
    place = lax.broadcasted_iota(jnp.int32, (128, SLOTS), 0)
    line = lax.broadcasted_iota(jnp.int32, (16, SLOTS), 0)
    group_of, low, point = slot_place(points[j])
    weight = slot_weight(j, weights)
    spread_out = jnp.zeros((16, SLOTS), F32)
    for c in range(3):
        spread_out = jnp.where(line == 3 * c + point, weight * got[c], spread_out)
    high = spread_out.astype(BF16)
    rest = (spread_out - high.astype(F32)).astype(BF16)
    zero = jnp.zeros((16, SLOTS), BF16)
    right = jnp.concatenate(
        [jnp.where(group_of == group, high, zero) for group in range(16)]
        + [jnp.where(group_of == group, rest, zero) for group in range(16)],
        axis=0,
    )
    chosen = jnp.where(place == low, 1.0, 0.0).astype(BF16)
    part = dot_nt(chosen, right)
    return part[:, 0:256] + part[:, 256:512]


def half_couple_kernel(got_mid, got_near, points, weights, stiffest, partial, most):
    partial[...] = sum_slots(1, got_mid, points, weights) + sum_slots(near_offset(), got_near, points, weights)
    most[...] = jnp.maximum(stiffest[...], jnp.broadcast_to(got_mid[3][:, 0:128], (8, 128)))


def couple_kernel(got_far, points, weights, partial, most, own, coupling, parcel, total):
    block = lax.axis_index("patch")
    blocks = lax.axis_size("patch")
    total[...] = partial[...] + sum_slots(2 - near_offset(), got_far, points, weights)
    lane = lax.broadcasted_iota(jnp.int32, (128, 128), 1)
    edges = []
    for group in range(16):
        half = total[:, (group // 8) * 128 : (group // 8) * 128 + 128]
        shift = (group % 8) * 16
        block_sum = pltpu.roll(half, 128 - shift, 1) if shift else half
        start = TOP + HALO + group * 128
        here = jnp.where(lane < 9, block_sum, 0.0) - own[group * 128 : group * 128 + 128, :]
        coupling[start : start + 128, :] = here
        if group == 0:
            edges.append(here[0:8, :])
        if group == 15:
            edges.append(here[120:128, :])
    lane_row = lax.broadcasted_iota(jnp.int32, (1, 128), 1)
    flat = []
    for edge in edges:
        line_up = edge[0:1, :]
        for row in range(1, 8):
            line_up = line_up + pltpu.roll(edge, 16 * row, 1)[row : row + 1, :]
        flat.append(jnp.where(lane_row == 15, most[0:1, :], line_up))
    parcel[...] = jnp.broadcast_to(flat[0][None], (blocks, 1, 128))
    parcel[jnp.minimum(block + 1, blocks - 1)] = flat[1]


def step_kernel(
    parcel, field, moving, outer, mass, thick, force, coupling_in, wide_a, wide_b, wide_c,
    new_field, new_moving, couple,
    state, speed, push, drag, operand_a, operand_b, place_out, speed_out, sem_out,
):
    block = lax.axis_index("patch")
    blocks = lax.axis_size("patch")
    fine = lax.axis_index("grp") == 1
    lane_row = lax.broadcasted_iota(jnp.int32, (1, 128), 1)
    sublane = lax.broadcasted_iota(jnp.int32, (8, 128), 0)
    most = jnp.max(parcel[...].reshape(blocks, 128), axis=0, keepdims=True)
    most = jnp.max(jnp.where(lane_row == 15, most, 0.0), axis=1, keepdims=True)
    limit = jnp.broadcast_to(most, (16, 128))
    base_step = COURANT * (1.0 / jnp.sqrt(limit))
    size = jnp.where(fine, base_step, SUBSTEPS * base_step)
    square = size * size
    inverse = 1.0 / size
    for start, there, exists in [
        (TOP, jnp.maximum(block - 1, 0), block > 0),
        (TOP + HALO + ROWS, jnp.minimum(block + 1, blocks - 1), block < blocks - 1),
    ]:
        line_up = jnp.broadcast_to(parcel[there], (8, 128))
        edge = line_up
        for row in range(1, 8):
            edge = jnp.where(sublane == row, pltpu.roll(line_up, 128 - 16 * row, 1), edge)
        edge = jnp.where(lax.broadcasted_iota(jnp.int32, (8, 128), 1) < 9, edge, 0.0)
        couple[start : start + 8, :] = jnp.where(exists, edge, 0.0)
    couple[0:TOP, :] = jnp.zeros((TOP, 128), F32)
    couple[PLANE - 8 : PLANE, :] = jnp.zeros((8, 128), F32)
    lane = lax.broadcasted_iota(jnp.int32, (16, 128), 1)

    def first_update(step, keep):
        for half in range(2):
            at = spread(2 * step + half)
            tile = pl.ds(step * 16, 16) if isinstance(step, int) else pl.ds(pl.multiple_of(step * 16, 16), 16)
            scaled = square * mass[0, at, :]
            pull = scaled * thick[0, at, :]
            both = couple[at, :]
            if keep:
                drag[half, tile, :] = pull
            for c in range(3):
                here = jnp.where(lane < 3, pltpu.roll(both, 128 - 3 * c, 1) if c else both, 0.0)
                drive = scaled * (outer[c, at, :] + here)
                new_speed = size * moving[c, at, :] + (drive - pull * force[half, tile, cols(c)])
                place = field[c, at, :] + new_speed
                if keep:
                    push[half, tile, cols(c)] = drive
                    speed[half, tile, cols(c)] = new_speed
                    state[half, tile, cols(c)] = place
                    operand_a[half, step * 16 + 16 : step * 16 + 32, cols(c)] = place.astype(BF16)
                else:
                    place_out[c, at, :] = place
                    speed_out[c, at, :] = new_speed * inverse

    @pl.when(jnp.logical_not(fine))
    def _():
        def some(turn, carry):
            for i in range(5):
                first_update(turn * 5 + i, False)
            return carry

        lax.fori_loop(0, PAIRS // 5, some, 0)

    def low_ends(operand):
        for c in range(3):
            operand[0, 0:16, cols(c)] = pltpu.roll(state[1, 63 * 16 : 64 * 16, cols(c)], 1, 0).astype(BF16)
            operand[1, 0:16, cols(c)] = pltpu.roll(state[0, 64 * 16 : 65 * 16, cols(c)], 1, 0).astype(BF16)

    def high_ends(operand):
        for c in range(3):
            operand[0, 66 * 16 : 67 * 16, cols(c)] = pltpu.roll(state[1, 0:16, cols(c)], 15, 0).astype(BF16)
            operand[1, 66 * 16 : 67 * 16, cols(c)] = pltpu.roll(state[0, 16:32, cols(c)], 15, 0).astype(BF16)

    def update(chunk, results, following):
        start = chunk * CHUNK
        rows = slice(start, start + CHUNK)
        for half in range(2):
            pull = drag[half, rows, :]
            for c in range(3):
                new_speed = speed[half, rows, cols(c)] + (push[half, rows, cols(c)] - pull * results[half][c])
                place = state[half, rows, cols(c)] + new_speed
                if following is not None:
                    speed[half, rows, cols(c)] = new_speed
                    state[half, rows, cols(c)] = place
                    following[half, start + 16 : start + 16 + CHUNK, cols(c)] = place.astype(BF16)
                else:
                    for i in range(CHUNK_PAIRS):
                        at = spread(2 * (start // 16 + i) + half)
                        place_out[c, at, :] = place[i * 16 : i * 16 + 16, :]
                        speed_out[c, at, :] = new_speed[i * 16 : i * 16 + 16, :] * inverse
        if following is not None and chunk == 0:
            high_ends(following)
        if following is not None and chunk == PAIR_ROWS // CHUNK - 1:
            low_ends(following)

    @pl.when(fine)
    def _():
        for step in [63, 64] + list(range(CHUNK_PAIRS + 1)):
            first_update(step, True)
        low_ends(operand_a)
        high_ends(operand_a)
        before = None
        for operand, following, order in [
            (operand_a, operand_b, [0, 1, 2, 3, 4]),
            (operand_b, operand_a, [1, 2, 3, 4, 0]),
            (operand_a, None, [2, 3, 4, 0, 1]),
        ]:
            for chunk in order:
                results = band_products(operand, chunk * CHUNK, CHUNK, wide_a, wide_b, wide_c)
                if operand is operand_a and following is operand_b:
                    first = (chunk + 1) * CHUNK_PAIRS + 1
                    for step in range(first, min(first + CHUNK_PAIRS, 63)):
                        first_update(step, True)
                if before is not None:
                    update(*before)
                before = (chunk, results, following)
        update(*before)

    out = []
    for c in range(3):
        inner = pl.ds(TOP + HALO, ROWS)
        out.append(
            pltpu.make_async_copy(place_out.at[c, inner, :], new_field.at[0, :, pl.ds(c * 128, 128)], sem_out.at[c])
        )
        out.append(
            pltpu.make_async_copy(speed_out.at[c, inner, :], new_moving.at[0, :, pl.ds(c * 128, 128)], sem_out.at[3 + c])
        )
    for copy in out:
        copy.start()
    for copy in out:
        copy.wait()


ANY = pl.BlockSpec(memory_space=pl.ANY)
IN_VMEM = pl.BlockSpec(memory_space=pltpu.VMEM)
DMA = pltpu.SemaphoreType.DMA
PLANE_3 = pltpu.VMEM((3, PLANE, 128), F32)
PLANE_1 = pltpu.VMEM((1, PLANE, 128), F32)
FULL = pltpu.VMEM((2, PAIR_ROWS, ROW), F32)
OPERAND = pltpu.VMEM((2, BAND_ROWS, ROW), BF16)
BANDS = [
    pltpu.VMEM((5 * ROW, 256), BF16),
    pltpu.VMEM((6 * ROW, 256), BF16),
    pltpu.VMEM((5 * ROW, 256), BF16),
]


def near(*arrays):
    return [pltpu.with_memory_space_constraint(a, pltpu.VMEM) for a in arrays]


def params(mib):
    return pltpu.CompilerParams(vmem_limit_bytes=mib * 2**20)


def per_device(
    displace, velocity, ext_force, inv_mass, thickness, stiff_bands, pair_points, pair_weights
):
    blocks = lax.axis_size("patch")
    points = pair_points.reshape(3, 1, SLOTS)
    weights = pair_weights.reshape(3, 1, SLOTS)
    near_pairs = [(i, i ^ 1) for i in range(blocks)]
    far_pairs = [(i, i + 1 if i % 2 else i - 1) for i in range(1, blocks - 1)]
    width = 3 * ROW + 2 * POINTS
    near_rows, far_rows = pl.pallas_call(
        bundle_kernel,
        out_shape=(pltpu.VMEM((HALO, width), F32), pltpu.VMEM((HALO, width), F32)),
        in_specs=[ANY] * 5,
        out_specs=[IN_VMEM] * 2,
        scratch_shapes=[DMA((10,))],
        compiler_params=params(2),
        name="bundle",
    )(*[pltpu.with_memory_space_constraint(a, pltpu.HBM) for a in [displace, velocity, ext_force, inv_mass, thickness]])
    far_rows = lax.ppermute(far_rows, "patch", far_pairs)

    field, operand, *bands, near_rows = pl.pallas_call(
        load_kernel,
        out_shape=(PLANE_3, OPERAND, *BANDS, pltpu.VMEM((HALO, width), F32)),
        in_specs=[ANY] * 2 + [IN_VMEM],
        out_specs=[IN_VMEM] * 6,
        input_output_aliases={2: 5},
        scratch_shapes=[DMA((3,)), DMA((20,))],
        compiler_params=params(2),
        name="load",
    )(displace, stiff_bands, *near(near_rows))
    near_rows = lax.ppermute(near_rows, "patch", near_pairs)

    plane = pltpu.VMEM((PLANE, 128), F32)
    tile = pltpu.VMEM((8, 128), F32)
    moving, outer, mass, thick, force, compact, stiffest = pl.pallas_call(
        force_kernel,
        out_shape=(PLANE_3, PLANE_3, PLANE_1, PLANE_1, FULL, plane, tile),
        in_specs=[IN_VMEM] * 5 + [ANY] * 4,
        out_specs=[IN_VMEM] * 7,
        scratch_shapes=[DMA((3,)), DMA((3,)), DMA((1,)), DMA((1,))],
        compiler_params=params(12),
        name="force",
    )(*near(field, operand, *bands), velocity, ext_force, inv_mass, thickness)

    slots = pltpu.VMEM((3, 1, SLOTS), F32)
    table = pltpu.VMEM((256, 256), BF16)
    field, operand, moving, outer, mass, thick, force, compact, table, send_far = pl.pallas_call(
        ends_kernel,
        out_shape=(PLANE_3, OPERAND, PLANE_3, PLANE_3, PLANE_1, PLANE_1, FULL, plane, table, pltpu.VMEM((FAR_ROWS, 1, SLOTS), F32)),
        in_specs=[IN_VMEM] * 14,
        out_specs=[IN_VMEM] * 10,
        input_output_aliases={i + 6: i for i in range(8)},
        compiler_params=params(12),
        name="ends",
    )(*near(*bands, near_rows, far_rows, points, field, operand, moving, outer, mass, thick, force, compact))

    both = ("grp", "patch")
    mid_pairs = [(i, i) for i in range(blocks)]

    def across(send, pairs):
        return lax.ppermute(
            send, both, [(g * blocks + i, (1 - g) * blocks + t) for g in range(2) for i, t in pairs]
        )

    got_far = across(send_far, far_pairs)
    send_mid, send_near = pl.pallas_call(
        pick_kernel,
        out_shape=(pltpu.VMEM((4, 1, SLOTS), F32), slots),
        in_specs=[IN_VMEM] * 3,
        out_specs=[IN_VMEM] * 2,
        compiler_params=params(12),
        cost_estimate=pl.CostEstimate(flops=1, transcendentals=0, bytes_accessed=1),
        name="pick",
    )(*near(table, points, stiffest))
    got_mid = across(send_mid, mid_pairs)
    got_near = across(send_near, near_pairs)
    own = pl.pallas_call(
        own_kernel,
        out_shape=pltpu.VMEM((ROWS, 128), F32),
        in_specs=[IN_VMEM] * 3,
        out_specs=IN_VMEM,
        scratch_shapes=[pltpu.VMEM((128, 256), F32)],
        compiler_params=params(12),
        name="own",
    )(*near(points, weights, compact))
    partial, most = pl.pallas_call(
        half_couple_kernel,
        out_shape=(pltpu.VMEM((128, 256), F32), tile),
        in_specs=[IN_VMEM] * 5,
        out_specs=[IN_VMEM] * 2,
        compiler_params=params(12),
        cost_estimate=pl.CostEstimate(flops=1, transcendentals=0, bytes_accessed=1),
        name="half_couple",
    )(*near(got_mid, got_near, points, weights, stiffest))
    coupling, parcel = pl.pallas_call(
        couple_kernel,
        out_shape=(plane, pltpu.VMEM((blocks, 1, 128), F32)),
        in_specs=[IN_VMEM] * 6,
        out_specs=[IN_VMEM] * 2,
        scratch_shapes=[pltpu.VMEM((128, 256), F32)],
        compiler_params=params(12),
        name="couple",
    )(*near(got_far, points, weights, partial, most, own))
    parcel = lax.all_to_all(parcel, "patch", 0, 0)

    new_field, new_moving, unused = pl.pallas_call(
        step_kernel,
        out_shape=(
            jax.ShapeDtypeStruct((1, ROWS, ROW), F32),
            jax.ShapeDtypeStruct((1, ROWS, ROW), F32),
            pltpu.VMEM((PLANE, 128), F32),
        ),
        in_specs=[IN_VMEM] * 11,
        out_specs=[ANY] * 2 + [IN_VMEM],
        input_output_aliases={7: 2},
        scratch_shapes=[FULL, FULL, FULL, pltpu.VMEM((2, PAIR_ROWS, 128), F32)]
        + [OPERAND, OPERAND, PLANE_3, PLANE_3, DMA((6,))],
        compiler_params=params(28),
        name="steps",
    )(*near(parcel, field, moving, outer, mass, thick, force, coupling, *bands))
    return new_field, new_moving


def solution(mesh):
    spec3 = P("grp", "patch", None)
    spec4 = P("grp", "patch", None, None)
    return jax.shard_map(
        per_device,
        mesh=mesh,
        in_specs=(spec3, spec3, spec3, spec3, spec3, P(), spec4, spec4),
        out_specs=(spec3, spec3),
        check_vma=False,
    )
```

```python
import jax
import jax.numpy as jnp
from jax import lax
from jax.experimental import pallas as pl
from jax.experimental.pallas import tpu as pltpu
from jax.sharding import PartitionSpec as P

POINTS = 128
REACH = 2
SUBSTEPS = 4
EDGE = 3
COURANT = 0.4
ROWS = 2048
ROW = 384
SLOTS = 1536
HALO = 8
RUN = 129
PAIRS = 65
PLANE = 2080
TOP = 8
PAIR_ROWS = PAIRS * 16
BAND_ROWS = (PAIRS + 2) * 16
CHUNK = 208
CHUNK_PAIRS = CHUNK // 16
EARLY = 4 * CHUNK_PAIRS
F32 = jnp.float32
BF16 = jnp.bfloat16


def dot(a, b):
    return jnp.dot(a, b, preferred_element_type=F32)


def dot_nt(a, b):
    return lax.dot_general(a, b, (((1,), (1,)), ((), ())), preferred_element_type=F32)


def cols(c):
    return slice(c * 128, (c + 1) * 128)


def band_copies(stiff, wide_a, wide_b, wide_c, sem):
    copies = []
    for b in range(5):
        rows = pl.ds(b * ROW, ROW)
        next_rows = pl.ds((b + 1) * ROW, ROW)
        copies.append((stiff.at[b, :, pl.ds(0, 256)], wide_a.at[rows, :]))
        copies.append((stiff.at[b, :, pl.ds(256, 128)], wide_b.at[rows, pl.ds(0, 128)]))
        copies.append((stiff.at[b, :, pl.ds(0, 128)], wide_b.at[next_rows, pl.ds(128, 128)]))
        copies.append((stiff.at[b, :, pl.ds(128, 256)], wide_c.at[rows, :]))
    return [pltpu.make_async_copy(src, dst, sem.at[i]) for i, (src, dst) in enumerate(copies)]


def band_zeros(wide_b):
    wide_b[5 * ROW : 6 * ROW, 0:128] = jnp.zeros((ROW, 128), BF16)
    wide_b[0:ROW, 128:256] = jnp.zeros((ROW, 128), BF16)


def pair_products(parts, wide_a, wide_b, wide_c):
    part_a = dot(jnp.concatenate(parts[:5], axis=1), wide_a[...])
    part_b = dot(jnp.concatenate(parts, axis=1), wide_b[...])
    part_c = dot(jnp.concatenate(parts[1:], axis=1), wide_c[...])
    even = [part_a[:, 0:128], part_a[:, 128:256], part_b[:, 0:128]]
    odd = [part_b[:, 128:256], part_c[:, 0:128], part_c[:, 128:256]]
    return even, odd


def band_products(operand, start, count, wide_a, wide_b, wide_c):
    parts = [operand[i % 2, pl.ds(start + (i // 2) * 16, count), :] for i in range(6)]
    return pair_products(parts, wide_a, wide_b, wide_c)


def put_halo(plane, near, far, even, first, count):
    for c in range(count):
        column = slice(first + c * 128, first + c * 128 + 128)
        plane[c, TOP : TOP + HALO, :] = jnp.where(even, far[:, column], near[:, column])
        plane[c, TOP + HALO + ROWS : TOP + 2 * HALO + ROWS, :] = jnp.where(even, near[:, column], far[:, column])
        plane[c, 0:TOP, :] = jnp.zeros((TOP, 128), F32)
        plane[c, PLANE - 8 : PLANE, :] = jnp.zeros((8, 128), F32)


def plane_copies(array, plane, count, sem):
    return [
        pltpu.make_async_copy(
            array.at[0, :, pl.ds(c * 128, 128)], plane.at[c, pl.ds(TOP + HALO, ROWS), :], sem.at[c]
        )
        for c in range(count)
    ]


def spread(k):
    return pl.ds(TOP + k, 16, stride=RUN)


def bundle_kernel(displace, velocity, ext_force, inv_mass, thickness, near_rows, far_rows, sem):
    even = lax.axis_index("patch") % 2 == 0
    copies = []
    last = ROWS - HALO
    near_start = pl.multiple_of(jnp.where(even, last, 0), 8)
    far_start = pl.multiple_of(jnp.where(even, 0, last), 8)
    column = 0
    for array in [displace, velocity, ext_force, inv_mass, thickness]:
        width = array.shape[2]
        for rows, out in [(far_start, far_rows), (near_start, near_rows)]:
            copies.append(
                pltpu.make_async_copy(
                    array.at[0, pl.ds(rows, HALO), :], out.at[:, pl.ds(column, width)], sem.at[len(copies)]
                )
            )
        column += width
    for copy in copies:
        copy.start()
    for copy in copies:
        copy.wait()


def fill_operand(field, operand, step):
    for half in range(2):
        for c in range(3):
            operand[half, pl.ds(step * 16, 16), cols(c)] = field[c, spread(2 * step + half - 2), :].astype(BF16)


def load_kernel(displace, stiff, near_in, field, operand, wide_a, wide_b, wide_c, near_rows, sem_field, sem_band):
    field_in = plane_copies(displace, field, 3, sem_field)
    bands_in = band_copies(stiff, wide_a, wide_b, wide_c, sem_band)
    for copy in field_in + bands_in:
        copy.start()
    for c in range(3):
        field[c, 0 : TOP + HALO, :] = jnp.zeros((TOP + HALO, 128), F32)
        field[c, TOP + HALO + ROWS : PLANE, :] = jnp.zeros((PLANE - TOP - HALO - ROWS, 128), F32)
    band_zeros(wide_b)
    for copy in field_in:
        copy.wait()

    def some(i, carry):
        for j in range(4):
            fill_operand(field, operand, pl.multiple_of(i * 4, 4) + j + 3)
        return carry

    for step in range(3):
        fill_operand(field, operand, step)
    lax.fori_loop(0, (PAIRS - 1) // 4, some, 0)
    for copy in bands_in:
        copy.wait()


def slot_place(entry):
    row = (entry * 21846) >> 16
    return row >> 7, row & 127, entry - 3 * row


def compact_rows(step, field, moving, thick, compact, force):
    lane = lax.broadcasted_iota(jnp.int32, (16, 128), 1)
    for half in range(2):
        at = spread(2 * step + half)
        half_thick = 0.5 * thick[0, at, :]
        parts = [field[c, at, :] + 0.5 * moving[c, at, :] + half_thick * force[half][c] for c in range(3)]
        compact[at, :] = jnp.where(
            lane < 3,
            parts[0],
            jnp.where(lane < 6, pltpu.roll(parts[1], 3, 1), pltpu.roll(parts[2], 6, 1)),
        )


def turn_rows(compact, table, groups):
    for group in groups:
        start = TOP + HALO + group * 128
        turned = compact[start : start + 128, :].T[0:16, :]
        upper = turned.astype(BF16)
        table[group * 16 : group * 16 + 16, 0:128] = upper
        table[group * 16 : group * 16 + 16, 128:256] = (turned - upper.astype(F32)).astype(BF16)


def some_rows(results, i):
    return [[part[i * 16 : i * 16 + 16, :] for part in half] for half in results]


def force_kernel(
    field, operand, wide_a, wide_b, wide_c, velocity, ext_force, inv_mass, thickness,
    moving, outer, mass, thick, force, compact, stiffest, table,
    sem_moving, sem_outer, sem_mass, sem_thick,
):
    thick_in = plane_copies(thickness, thick, 1, sem_thick)
    moving_in = plane_copies(velocity, moving, 3, sem_moving)
    mass_in = plane_copies(inv_mass, mass, 1, sem_mass)
    outer_in = plane_copies(ext_force, outer, 3, sem_outer)
    for copy in thick_in + moving_in + mass_in + outer_in:
        copy.start()

    def make_compact(start, results):
        for i in range(CHUNK_PAIRS):
            compact_rows(start // 16 + i, field, moving, thick, compact, some_rows(results, i))

    before = None
    for start in range(0, PAIR_ROWS, CHUNK):
        results = band_products(operand, start, CHUNK, wide_a, wide_b, wide_c)
        for half in range(2):
            for c in range(3):
                force[half, start : start + CHUNK, cols(c)] = results[half][c]
        if before is None:
            for copy in thick_in + moving_in:
                copy.wait()
        else:
            make_compact(*before)
        before = (start, results)
    for copy in mass_in:
        copy.wait()
    product = jnp.zeros((8, 128), F32)
    for i in range(8):
        rows = slice(TOP + HALO + i * 256, TOP + HALO + i * 256 + 256)
        product = jnp.maximum(
            product, jnp.max((mass[0, rows, :] * thick[0, rows, :]).reshape(32, 8, 128), axis=0)
        )
    most = jnp.max(jnp.max(product, axis=0, keepdims=True), axis=1, keepdims=True)
    stiffest[...] = jnp.broadcast_to(most, (8, 128))
    make_compact(*before)
    turn_rows(compact, table, range(1, 15))
    for copy in outer_in:
        copy.wait()


def pick_slots(entry, table, send):
    place = lax.broadcasted_iota(jnp.int32, (128, SLOTS), 0)
    group_of, low, point = slot_place(entry)
    chosen = jnp.where(place == low, 1.0, 0.0).astype(BF16)
    picked = dot(table[...], jnp.concatenate([chosen, chosen], axis=0))
    total = jnp.zeros((16, SLOTS), F32)
    for group in range(16):
        total = total + jnp.where(group_of == group, picked[group * 16 : group * 16 + 16, :], 0.0)
    for c in range(3):
        send[c] = jnp.where(
            point == 0,
            total[3 * c : 3 * c + 1, :],
            jnp.where(point == 1, total[3 * c + 1 : 3 * c + 2, :], total[3 * c + 2 : 3 * c + 3, :]),
        )


def near_offset():
    return jnp.where(lax.axis_index("patch") % 2 == 0, 2, 0)


FAR_ROWS = 5
LOW_PAIRS = 5
HIGH_PAIR = 59


def ends_kernel(
    wide_a, wide_b, wide_c, near_rows, far_rows, points,
    field_in, operand_in, moving_in, outer_in, mass_in, thick_in, force_in, compact_in, table_in,
    field, operand, moving, outer, mass, thick, force, compact, table, send_far,
):
    even = lax.axis_index("patch") % 2 == 0
    put_halo(field, near_rows, far_rows, even, 0, 3)
    put_halo(moving, near_rows, far_rows, even, 384, 3)
    put_halo(outer, near_rows, far_rows, even, 768, 3)
    put_halo(mass, near_rows, far_rows, even, 1152, 1)
    put_halo(thick, near_rows, far_rows, even, 1280, 1)
    for step in list(range(6)) + list(range(60, 67)):
        fill_operand(field, operand, step)
    low = LOW_PAIRS * 16
    high = (PAIRS - HIGH_PAIR) * 16
    parts = [
        jnp.concatenate(
            [
                operand[i % 2, (i // 2) * 16 : (i // 2) * 16 + low, :],
                operand[i % 2, (HIGH_PAIR + i // 2) * 16 : (HIGH_PAIR + i // 2) * 16 + high, :],
            ],
            axis=0,
        )
        for i in range(6)
    ]
    results = pair_products(parts, wide_a, wide_b, wide_c)
    for half in range(2):
        for c in range(3):
            force[half, 0:low, cols(c)] = results[half][c][:low]
            force[half, HIGH_PAIR * 16 : PAIR_ROWS, cols(c)] = results[half][c][low:]
    for i, step in enumerate(list(range(LOW_PAIRS)) + list(range(HIGH_PAIR, PAIRS))):
        compact_rows(step, field, moving, thick, compact, some_rows(results, i))
    turn_rows(compact, table, [0, 15])
    pick_slots(points[2 - near_offset()], table, send_far)
    for c in range(3, FAR_ROWS):
        send_far[c] = jnp.zeros((1, SLOTS), F32)


def pick_kernel(table, points, stiffest, send_mid, send_near):
    send_mid[3] = jnp.concatenate([stiffest[0:1, :]] * (SLOTS // 128), axis=1)
    pick_slots(points[1], table, send_mid)
    pick_slots(points[near_offset()], table, send_near)


def slot_weight(j, weights):
    neighbour = lax.axis_index("patch") + (j - 1)
    present = jnp.where((neighbour >= 0) & (neighbour < lax.axis_size("patch")), 1.0, 0.0)
    return weights[j] * present


def own_kernel(points, weights, compact, own, total):
    place = lax.broadcasted_iota(jnp.int32, (128, SLOTS), 0)
    line = lax.broadcasted_iota(jnp.int32, (16, SLOTS), 0)
    summed = None
    for j in range(3):
        group_of, low, point = slot_place(points[j])
        weight = slot_weight(j, weights)
        upper = weight.astype(BF16).astype(F32)
        both = jnp.where(line == point, upper, jnp.where(line == point + 8, weight - upper, 0.0)).astype(BF16)
        zero = jnp.zeros((16, SLOTS), BF16)
        right = jnp.concatenate([jnp.where(group_of == group, both, zero) for group in range(16)], axis=0)
        part = dot_nt(jnp.where(place == low, 1.0, 0.0).astype(BF16), right)
        summed = part if summed is None else summed + part
    total[...] = summed
    lane = lax.broadcasted_iota(jnp.int32, (128, 128), 1)
    for group in range(16):
        half = total[:, (group // 8) * 128 : (group // 8) * 128 + 128]
        half = half + pltpu.roll(half, 120, 1)
        shift = (group % 8) * 16
        weight_sum = jnp.where(
            lane < 3,
            pltpu.roll(half, 128 - shift, 1) if shift else half,
            jnp.where(
                lane < 6,
                pltpu.roll(half, (131 - shift) % 128, 1),
                pltpu.roll(half, (134 - shift) % 128, 1),
            ),
        )
        start = TOP + HALO + group * 128
        own[group * 128 : group * 128 + 128, :] = jnp.where(
            lane < 9, compact[start : start + 128, :] * weight_sum, 0.0
        )


def sum_slots(j, got, points, weights):
    place = lax.broadcasted_iota(jnp.int32, (128, SLOTS), 0)
    line = lax.broadcasted_iota(jnp.int32, (16, SLOTS), 0)
    group_of, low, point = slot_place(points[j])
    weight = slot_weight(j, weights)
    spread_out = jnp.zeros((16, SLOTS), F32)
    for c in range(3):
        spread_out = jnp.where(line == 3 * c + point, weight * got[c], spread_out)
    high = spread_out.astype(BF16)
    rest = (spread_out - high.astype(F32)).astype(BF16)
    zero = jnp.zeros((16, SLOTS), BF16)
    right = jnp.concatenate(
        [jnp.where(group_of == group, high, zero) for group in range(16)]
        + [jnp.where(group_of == group, rest, zero) for group in range(16)],
        axis=0,
    )
    chosen = jnp.where(place == low, 1.0, 0.0).astype(BF16)
    part = dot_nt(chosen, right)
    return part[:, 0:256] + part[:, 256:512]


def half_couple_kernel(got_mid, got_near, points, weights, stiffest, partial, most):
    partial[...] = sum_slots(1, got_mid, points, weights) + sum_slots(near_offset(), got_near, points, weights)
    most[...] = jnp.maximum(stiffest[...], jnp.broadcast_to(got_mid[3][:, 0:128], (8, 128)))


def couple_kernel(got_far, points, weights, partial, most, own, coupling, parcel, total):
    block = lax.axis_index("patch")
    blocks = lax.axis_size("patch")
    total[...] = partial[...] + sum_slots(2 - near_offset(), got_far, points, weights)
    lane = lax.broadcasted_iota(jnp.int32, (128, 128), 1)
    edges = []
    for group in range(16):
        half = total[:, (group // 8) * 128 : (group // 8) * 128 + 128]
        shift = (group % 8) * 16
        block_sum = pltpu.roll(half, 128 - shift, 1) if shift else half
        start = TOP + HALO + group * 128
        here = jnp.where(lane < 9, block_sum, 0.0) - own[group * 128 : group * 128 + 128, :]
        coupling[start : start + 128, :] = here
        if group == 0:
            edges.append(here[0:8, :])
        if group == 15:
            edges.append(here[120:128, :])
    lane_row = lax.broadcasted_iota(jnp.int32, (1, 128), 1)
    flat = []
    for edge in edges:
        line_up = edge[0:1, :]
        for row in range(1, 8):
            line_up = line_up + pltpu.roll(edge, 16 * row, 1)[row : row + 1, :]
        flat.append(jnp.where(lane_row == 15, most[0:1, :], line_up))
    parcel[...] = jnp.broadcast_to(flat[0][None], (blocks, 1, 128))
    parcel[jnp.minimum(block + 1, blocks - 1)] = flat[1]


def step_kernel(
    parcel, field, moving, outer, mass, thick, force, coupling_in, wide_a, wide_b, wide_c,
    new_field, new_moving, couple,
    state, speed, push, drag, operand_a, operand_b, place_out, speed_out, place_late, speed_late, sem_out, sem_late,
):
    block = lax.axis_index("patch")
    blocks = lax.axis_size("patch")
    fine = lax.axis_index("grp") == 1
    lane_row = lax.broadcasted_iota(jnp.int32, (1, 128), 1)
    sublane = lax.broadcasted_iota(jnp.int32, (8, 128), 0)
    most = jnp.max(parcel[...].reshape(blocks, 128), axis=0, keepdims=True)
    most = jnp.max(jnp.where(lane_row == 15, most, 0.0), axis=1, keepdims=True)
    limit = jnp.broadcast_to(most, (16, 128))
    base_step = COURANT * (1.0 / jnp.sqrt(limit))
    size = jnp.where(fine, base_step, SUBSTEPS * base_step)
    square = size * size
    inverse = 1.0 / size
    for start, there, exists in [
        (TOP, jnp.maximum(block - 1, 0), block > 0),
        (TOP + HALO + ROWS, jnp.minimum(block + 1, blocks - 1), block < blocks - 1),
    ]:
        line_up = jnp.broadcast_to(parcel[there], (8, 128))
        edge = line_up
        for row in range(1, 8):
            edge = jnp.where(sublane == row, pltpu.roll(line_up, 128 - 16 * row, 1), edge)
        edge = jnp.where(lax.broadcasted_iota(jnp.int32, (8, 128), 1) < 9, edge, 0.0)
        couple[start : start + 8, :] = jnp.where(exists, edge, 0.0)
    couple[0:TOP, :] = jnp.zeros((TOP, 128), F32)
    couple[PLANE - 8 : PLANE, :] = jnp.zeros((8, 128), F32)
    lane = lax.broadcasted_iota(jnp.int32, (16, 128), 1)

    def first_update(step, keep):
        for half in range(2):
            at = spread(2 * step + half)
            tile = pl.ds(step * 16, 16) if isinstance(step, int) else pl.ds(pl.multiple_of(step * 16, 16), 16)
            scaled = square * mass[0, at, :]
            pull = scaled * thick[0, at, :]
            both = couple[at, :]
            if keep:
                drag[half, tile, :] = pull
            for c in range(3):
                here = jnp.where(lane < 3, pltpu.roll(both, 128 - 3 * c, 1) if c else both, 0.0)
                drive = scaled * (outer[c, at, :] + here)
                new_speed = size * moving[c, at, :] + (drive - pull * force[half, tile, cols(c)])
                place = field[c, at, :] + new_speed
                if keep:
                    push[half, tile, cols(c)] = drive
                    speed[half, tile, cols(c)] = new_speed
                    state[half, tile, cols(c)] = place
                    operand_a[half, step * 16 + 16 : step * 16 + 32, cols(c)] = place.astype(BF16)
                else:
                    place_out[c, at, :] = place
                    speed_out[c, at, :] = new_speed * inverse

    @pl.when(jnp.logical_not(fine))
    def _():
        def some(turn, carry):
            for i in range(5):
                first_update(turn * 5 + i, False)
            return carry

        lax.fori_loop(0, PAIRS // 5, some, 0)
        out = []
        for c in range(3):
            inner = pl.ds(TOP + HALO, ROWS)
            out.append(
                pltpu.make_async_copy(place_out.at[c, inner, :], new_field.at[0, :, pl.ds(c * 128, 128)], sem_out.at[c])
            )
            out.append(
                pltpu.make_async_copy(speed_out.at[c, inner, :], new_moving.at[0, :, pl.ds(c * 128, 128)], sem_out.at[3 + c])
            )
        for copy in out:
            copy.start()
        for copy in out:
            copy.wait()

    def low_ends(operand):
        for c in range(3):
            operand[0, 0:16, cols(c)] = pltpu.roll(state[1, 63 * 16 : 64 * 16, cols(c)], 1, 0).astype(BF16)
            operand[1, 0:16, cols(c)] = pltpu.roll(state[0, 64 * 16 : 65 * 16, cols(c)], 1, 0).astype(BF16)

    def high_ends(operand):
        for c in range(3):
            operand[0, 66 * 16 : 67 * 16, cols(c)] = pltpu.roll(state[1, 0:16, cols(c)], 15, 0).astype(BF16)
            operand[1, 66 * 16 : 67 * 16, cols(c)] = pltpu.roll(state[0, 16:32, cols(c)], 15, 0).astype(BF16)

    def update(chunk, results, following):
        start = chunk * CHUNK
        rows = slice(start, start + CHUNK)
        for half in range(2):
            pull = drag[half, rows, :]
            for c in range(3):
                new_speed = speed[half, rows, cols(c)] + (push[half, rows, cols(c)] - pull * results[half][c])
                place = state[half, rows, cols(c)] + new_speed
                if following is not None:
                    speed[half, rows, cols(c)] = new_speed
                    state[half, rows, cols(c)] = place
                    following[half, start + 16 : start + 16 + CHUNK, cols(c)] = place.astype(BF16)
                else:
                    for i in range(CHUNK_PAIRS):
                        k = 2 * (start // 16 + i) + half
                        some_place = place[i * 16 : i * 16 + 16, :]
                        some_speed = new_speed[i * 16 : i * 16 + 16, :] * inverse
                        if k >= EARLY:
                            place_out[c, spread(k), :] = some_place
                            speed_out[c, spread(k), :] = some_speed
                        if k < EARLY + 8 or RUN - 9 <= k < RUN:
                            place_late[c, spread(k), :] = some_place
                            speed_late[c, spread(k), :] = some_speed
        if following is not None and chunk == 0:
            high_ends(following)
        if following is not None and chunk == PAIR_ROWS // CHUNK - 1:
            low_ends(following)

    @pl.when(fine)
    def _():
        for step in [63, 64] + list(range(CHUNK_PAIRS + 1)):
            first_update(step, True)
        low_ends(operand_a)
        high_ends(operand_a)
        pieces = []
        done = 0
        for run in range(16):
            begin = (run * RUN + EARLY - HALO + 7) // 8 * 8
            end = min((run * RUN + RUN - HALO) // 8 * 8, ROWS)
            pieces.append((done, begin, end))
            done = end
        assert done == ROWS
        targets = [(place_out, place_late, new_field), (speed_out, speed_late, new_moving)]

        def copies(late, rows):
            made = []
            for i, pair in enumerate(targets):
                for c in range(3):
                    for first, count in rows:
                        made.append(
                            pltpu.make_async_copy(
                                pair[late].at[c, pl.ds(TOP + HALO + first, count), :],
                                pair[2].at[0, pl.ds(first, count), pl.ds(c * 128, 128)],
                                (sem_late if late else sem_out).at[3 * i + c],
                            )
                        )
            return made

        early_rows = [(begin, end - begin) for _, begin, end in pieces]
        late_rows = [(gap, begin - gap) for gap, begin, _ in pieces]
        before = None
        for operand, following, order in [
            (operand_a, operand_b, [0, 1, 2, 3, 4]),
            (operand_b, operand_a, [1, 2, 3, 4, 0]),
            (operand_a, None, [2, 3, 4, 0, 1]),
        ]:
            for chunk in order:
                results = band_products(operand, chunk * CHUNK, CHUNK, wide_a, wide_b, wide_c)
                if operand is operand_a and following is operand_b:
                    first = (chunk + 1) * CHUNK_PAIRS + 1
                    for step in range(first, min(first + CHUNK_PAIRS, 63)):
                        first_update(step, True)
                if before is not None:
                    update(*before)
                    if before[0] == 4 and before[2] is None:
                        for copy in copies(0, early_rows):
                            copy.start()
                before = (chunk, results, following)
        update(*before)
        for copy in copies(1, late_rows):
            copy.start()
        for late, rows in enumerate([early_rows, late_rows]):
            for copy in copies(late, [(0, sum(count for _, count in rows))]):
                copy.wait()


ANY = pl.BlockSpec(memory_space=pl.ANY)
IN_VMEM = pl.BlockSpec(memory_space=pltpu.VMEM)
DMA = pltpu.SemaphoreType.DMA
PLANE_3 = pltpu.VMEM((3, PLANE, 128), F32)
PLANE_1 = pltpu.VMEM((1, PLANE, 128), F32)
FULL = pltpu.VMEM((2, PAIR_ROWS, ROW), F32)
OPERAND = pltpu.VMEM((2, BAND_ROWS, ROW), BF16)
BANDS = [
    pltpu.VMEM((5 * ROW, 256), BF16),
    pltpu.VMEM((6 * ROW, 256), BF16),
    pltpu.VMEM((5 * ROW, 256), BF16),
]


def near(*arrays):
    return [pltpu.with_memory_space_constraint(a, pltpu.VMEM) for a in arrays]


def params(mib):
    return pltpu.CompilerParams(vmem_limit_bytes=mib * 2**20)


def per_device(
    displace, velocity, ext_force, inv_mass, thickness, stiff_bands, pair_points, pair_weights
):
    blocks = lax.axis_size("patch")
    points = pair_points.reshape(3, 1, SLOTS)
    weights = pair_weights.reshape(3, 1, SLOTS)
    near_pairs = [(i, i ^ 1) for i in range(blocks)]
    far_pairs = [(i, i + 1 if i % 2 else i - 1) for i in range(1, blocks - 1)]
    width = 3 * ROW + 2 * POINTS
    near_rows, far_rows = pl.pallas_call(
        bundle_kernel,
        out_shape=(pltpu.VMEM((HALO, width), F32), pltpu.VMEM((HALO, width), F32)),
        in_specs=[ANY] * 5,
        out_specs=[IN_VMEM] * 2,
        scratch_shapes=[DMA((10,))],
        compiler_params=params(2),
        name="bundle",
    )(*[pltpu.with_memory_space_constraint(a, pltpu.HBM) for a in [displace, velocity, ext_force, inv_mass, thickness]])
    far_rows = lax.ppermute(far_rows, "patch", far_pairs)

    field, operand, *bands, near_rows = pl.pallas_call(
        load_kernel,
        out_shape=(PLANE_3, OPERAND, *BANDS, pltpu.VMEM((HALO, width), F32)),
        in_specs=[ANY] * 2 + [IN_VMEM],
        out_specs=[IN_VMEM] * 6,
        input_output_aliases={2: 5},
        scratch_shapes=[DMA((3,)), DMA((20,))],
        compiler_params=params(2),
        name="load",
    )(displace, stiff_bands, *near(near_rows))
    near_rows = lax.ppermute(near_rows, "patch", near_pairs)

    plane = pltpu.VMEM((PLANE, 128), F32)
    tile = pltpu.VMEM((8, 128), F32)
    table = pltpu.VMEM((256, 256), BF16)
    moving, outer, mass, thick, force, compact, stiffest, turned = pl.pallas_call(
        force_kernel,
        out_shape=(PLANE_3, PLANE_3, PLANE_1, PLANE_1, FULL, plane, tile, table),
        in_specs=[IN_VMEM] * 5 + [ANY] * 4,
        out_specs=[IN_VMEM] * 8,
        scratch_shapes=[DMA((3,)), DMA((3,)), DMA((1,)), DMA((1,))],
        compiler_params=params(12),
        name="force",
    )(*near(field, operand, *bands), velocity, ext_force, inv_mass, thickness)

    slots = pltpu.VMEM((3, 1, SLOTS), F32)
    field, operand, moving, outer, mass, thick, force, compact, table, send_far = pl.pallas_call(
        ends_kernel,
        out_shape=(PLANE_3, OPERAND, PLANE_3, PLANE_3, PLANE_1, PLANE_1, FULL, plane, table, pltpu.VMEM((FAR_ROWS, 1, SLOTS), F32)),
        in_specs=[IN_VMEM] * 15,
        out_specs=[IN_VMEM] * 10,
        input_output_aliases={i + 6: i for i in range(9)},
        compiler_params=params(12),
        name="ends",
    )(*near(*bands, near_rows, far_rows, points, field, operand, moving, outer, mass, thick, force, compact, turned))

    both = ("grp", "patch")
    mid_pairs = [(i, i) for i in range(blocks)]

    def across(send, pairs):
        return lax.ppermute(
            send, both, [(g * blocks + i, (1 - g) * blocks + t) for g in range(2) for i, t in pairs]
        )

    got_far = across(send_far, far_pairs)
    send_mid, send_near = pl.pallas_call(
        pick_kernel,
        out_shape=(pltpu.VMEM((4, 1, SLOTS), F32), slots),
        in_specs=[IN_VMEM] * 3,
        out_specs=[IN_VMEM] * 2,
        compiler_params=params(12),
        cost_estimate=pl.CostEstimate(flops=1, transcendentals=0, bytes_accessed=1),
        name="pick",
    )(*near(table, points, stiffest))
    got_mid = across(send_mid, mid_pairs)
    got_near = across(send_near, near_pairs)
    own = pl.pallas_call(
        own_kernel,
        out_shape=pltpu.VMEM((ROWS, 128), F32),
        in_specs=[IN_VMEM] * 3,
        out_specs=IN_VMEM,
        scratch_shapes=[pltpu.VMEM((128, 256), F32)],
        compiler_params=params(12),
        name="own",
    )(*near(points, weights, compact))
    partial, most = pl.pallas_call(
        half_couple_kernel,
        out_shape=(pltpu.VMEM((128, 256), F32), tile),
        in_specs=[IN_VMEM] * 5,
        out_specs=[IN_VMEM] * 2,
        compiler_params=params(12),
        cost_estimate=pl.CostEstimate(flops=1, transcendentals=0, bytes_accessed=1),
        name="half_couple",
    )(*near(got_mid, got_near, points, weights, stiffest))
    coupling, parcel = pl.pallas_call(
        couple_kernel,
        out_shape=(plane, pltpu.VMEM((blocks, 1, 128), F32)),
        in_specs=[IN_VMEM] * 6,
        out_specs=[IN_VMEM] * 2,
        scratch_shapes=[pltpu.VMEM((128, 256), F32)],
        compiler_params=params(12),
        name="couple",
    )(*near(got_far, points, weights, partial, most, own))
    parcel = lax.all_to_all(parcel, "patch", 0, 0)

    new_field, new_moving, unused = pl.pallas_call(
        step_kernel,
        out_shape=(
            jax.ShapeDtypeStruct((1, ROWS, ROW), F32),
            jax.ShapeDtypeStruct((1, ROWS, ROW), F32),
            pltpu.VMEM((PLANE, 128), F32),
        ),
        in_specs=[IN_VMEM] * 11,
        out_specs=[ANY] * 2 + [IN_VMEM],
        input_output_aliases={7: 2},
        scratch_shapes=[FULL, FULL, FULL, pltpu.VMEM((2, PAIR_ROWS, 128), F32)]
        + [OPERAND, OPERAND, PLANE_3, PLANE_3, PLANE_3, PLANE_3, DMA((6,)), DMA((6,))],
        compiler_params=params(35),
        name="steps",
    )(*near(parcel, field, moving, outer, mass, thick, force, coupling, *bands))
    return new_field, new_moving


def solution(mesh):
    spec3 = P("grp", "patch", None)
    spec4 = P("grp", "patch", None, None)
    return jax.shard_map(
        per_device,
        mesh=mesh,
        in_specs=(spec3, spec3, spec3, spec3, spec3, P(), spec4, spec4),
        out_specs=(spec3, spec3),
        check_vma=False,
    )
```

```python
import jax
import jax.numpy as jnp
from jax import lax
from jax.experimental import pallas as pl
from jax.experimental.pallas import tpu as pltpu
from jax.sharding import PartitionSpec as P

POINTS = 128
REACH = 2
SUBSTEPS = 4
EDGE = 3
COURANT = 0.4
ROWS = 2048
ROW = 384
SLOTS = 1536
HALO = 8
RUN = 129
PAIRS = 65
PLANE = 2080
TOP = 8
PAIR_ROWS = PAIRS * 16
BAND_ROWS = (PAIRS + 2) * 16
CHUNK = 208
CHUNK_PAIRS = CHUNK // 16
EARLY = 4 * CHUNK_PAIRS
F32 = jnp.float32
BF16 = jnp.bfloat16


def dot(a, b):
    return jnp.dot(a, b, preferred_element_type=F32)


def dot_nt(a, b):
    return lax.dot_general(a, b, (((1,), (1,)), ((), ())), preferred_element_type=F32)


def cols(c):
    return slice(c * 128, (c + 1) * 128)


def band_copies(stiff, wide_a, wide_b, wide_c, sem):
    copies = []
    for b in range(5):
        rows = pl.ds(b * ROW, ROW)
        next_rows = pl.ds((b + 1) * ROW, ROW)
        copies.append((stiff.at[b, :, pl.ds(0, 256)], wide_a.at[rows, :]))
        copies.append((stiff.at[b, :, pl.ds(256, 128)], wide_b.at[rows, pl.ds(0, 128)]))
        copies.append((stiff.at[b, :, pl.ds(0, 128)], wide_b.at[next_rows, pl.ds(128, 128)]))
        copies.append((stiff.at[b, :, pl.ds(128, 256)], wide_c.at[rows, :]))
    return [pltpu.make_async_copy(src, dst, sem.at[i]) for i, (src, dst) in enumerate(copies)]


def band_zeros(wide_b):
    wide_b[5 * ROW : 6 * ROW, 0:128] = jnp.zeros((ROW, 128), BF16)
    wide_b[0:ROW, 128:256] = jnp.zeros((ROW, 128), BF16)


def pair_products(parts, wide_a, wide_b, wide_c):
    part_a = dot(jnp.concatenate(parts[:5], axis=1), wide_a[...])
    part_b = dot(jnp.concatenate(parts, axis=1), wide_b[...])
    part_c = dot(jnp.concatenate(parts[1:], axis=1), wide_c[...])
    even = [part_a[:, 0:128], part_a[:, 128:256], part_b[:, 0:128]]
    odd = [part_b[:, 128:256], part_c[:, 0:128], part_c[:, 128:256]]
    return even, odd


def band_products(operand, start, count, wide_a, wide_b, wide_c):
    parts = [operand[i % 2, pl.ds(start + (i // 2) * 16, count), :] for i in range(6)]
    return pair_products(parts, wide_a, wide_b, wide_c)


def put_halo(plane, near, far, even, first, count):
    for c in range(count):
        column = slice(first + c * 128, first + c * 128 + 128)
        plane[c, TOP : TOP + HALO, :] = jnp.where(even, far[:, column], near[:, column])
        plane[c, TOP + HALO + ROWS : TOP + 2 * HALO + ROWS, :] = jnp.where(even, near[:, column], far[:, column])
        plane[c, 0:TOP, :] = jnp.zeros((TOP, 128), F32)
        plane[c, PLANE - 8 : PLANE, :] = jnp.zeros((8, 128), F32)


def plane_copies(array, plane, count, sem):
    return [
        pltpu.make_async_copy(
            array.at[0, :, pl.ds(c * 128, 128)], plane.at[c, pl.ds(TOP + HALO, ROWS), :], sem.at[c]
        )
        for c in range(count)
    ]


def spread(k):
    return pl.ds(TOP + k, 16, stride=RUN)


def bundle_kernel(displace, velocity, ext_force, inv_mass, thickness, near_rows, far_rows, sem):
    even = lax.axis_index("patch") % 2 == 0
    copies = []
    last = ROWS - HALO
    near_start = pl.multiple_of(jnp.where(even, last, 0), 8)
    far_start = pl.multiple_of(jnp.where(even, 0, last), 8)
    column = 0
    for array in [displace, velocity, ext_force, inv_mass, thickness]:
        width = array.shape[2]
        for rows, out in [(far_start, far_rows), (near_start, near_rows)]:
            copies.append(
                pltpu.make_async_copy(
                    array.at[0, pl.ds(rows, HALO), :], out.at[:, pl.ds(column, width)], sem.at[len(copies)]
                )
            )
        column += width
    for copy in copies:
        copy.start()
    for copy in copies:
        copy.wait()


def fill_operand(field, operand, step):
    for half in range(2):
        for c in range(3):
            operand[half, pl.ds(step * 16, 16), cols(c)] = field[c, spread(2 * step + half - 2), :].astype(BF16)


def load_kernel(displace, stiff, near_in, field, operand, wide_a, wide_b, wide_c, near_rows, sem_field, sem_band):
    field_in = plane_copies(displace, field, 3, sem_field)
    bands_in = band_copies(stiff, wide_a, wide_b, wide_c, sem_band)
    for copy in field_in + bands_in:
        copy.start()
    for c in range(3):
        field[c, 0 : TOP + HALO, :] = jnp.zeros((TOP + HALO, 128), F32)
        field[c, TOP + HALO + ROWS : PLANE, :] = jnp.zeros((PLANE - TOP - HALO - ROWS, 128), F32)
    band_zeros(wide_b)
    for copy in field_in:
        copy.wait()

    def some(i, carry):
        for j in range(4):
            fill_operand(field, operand, pl.multiple_of(i * 4, 4) + j + 3)
        return carry

    for step in range(3):
        fill_operand(field, operand, step)
    lax.fori_loop(0, (PAIRS - 1) // 4, some, 0)
    for copy in bands_in:
        copy.wait()


def slot_place(entry):
    row = (entry * 21846) >> 16
    return row >> 7, row & 127, entry - 3 * row


def compact_rows(step, field, moving, thick, compact, force):
    lane = lax.broadcasted_iota(jnp.int32, (16, 128), 1)
    for half in range(2):
        at = spread(2 * step + half)
        half_thick = 0.5 * thick[0, at, :]
        parts = [field[c, at, :] + 0.5 * moving[c, at, :] + half_thick * force[half][c] for c in range(3)]
        compact[at, :] = jnp.where(
            lane < 3,
            parts[0],
            jnp.where(lane < 6, pltpu.roll(parts[1], 3, 1), pltpu.roll(parts[2], 6, 1)),
        )


def turn_rows(compact, table, groups):
    for group in groups:
        start = TOP + HALO + group * 128
        turned = compact[start : start + 128, :].T[0:16, :]
        upper = turned.astype(BF16)
        table[group * 16 : group * 16 + 16, 0:128] = upper
        table[group * 16 : group * 16 + 16, 128:256] = (turned - upper.astype(F32)).astype(BF16)


def some_rows(results, i):
    return [[part[i * 16 : i * 16 + 16, :] for part in half] for half in results]


def force_kernel(
    field, operand, wide_a, wide_b, wide_c, velocity, ext_force, inv_mass, thickness,
    moving, outer, mass, thick, force, compact, stiffest, table,
    sem_moving, sem_outer, sem_mass, sem_thick,
):
    thick_in = plane_copies(thickness, thick, 1, sem_thick)
    moving_in = plane_copies(velocity, moving, 3, sem_moving)
    mass_in = plane_copies(inv_mass, mass, 1, sem_mass)
    outer_in = plane_copies(ext_force, outer, 3, sem_outer)
    for copy in thick_in + moving_in + mass_in + outer_in:
        copy.start()

    def make_compact(start, results):
        for i in range(CHUNK_PAIRS):
            compact_rows(start // 16 + i, field, moving, thick, compact, some_rows(results, i))

    before = None
    for start in range(0, PAIR_ROWS, CHUNK):
        results = band_products(operand, start, CHUNK, wide_a, wide_b, wide_c)
        for half in range(2):
            for c in range(3):
                force[half, start : start + CHUNK, cols(c)] = results[half][c]
        if before is None:
            for copy in thick_in + moving_in:
                copy.wait()
        else:
            make_compact(*before)
        before = (start, results)
    for copy in mass_in:
        copy.wait()
    product = jnp.zeros((8, 128), F32)
    for i in range(8):
        rows = slice(TOP + HALO + i * 256, TOP + HALO + i * 256 + 256)
        product = jnp.maximum(
            product, jnp.max((mass[0, rows, :] * thick[0, rows, :]).reshape(32, 8, 128), axis=0)
        )
    most = jnp.max(jnp.max(product, axis=0, keepdims=True), axis=1, keepdims=True)
    stiffest[...] = jnp.broadcast_to(most, (8, 128))
    make_compact(*before)
    turn_rows(compact, table, range(1, 15))
    for copy in outer_in:
        copy.wait()


def pick_slots(entry, table, send):
    place = lax.broadcasted_iota(jnp.int32, (128, SLOTS), 0)
    group_of, low, point = slot_place(entry)
    chosen = jnp.where(place == low, 1.0, 0.0).astype(BF16)
    picked = dot(table[...], jnp.concatenate([chosen, chosen], axis=0))
    total = jnp.zeros((16, SLOTS), F32)
    for group in range(16):
        total = total + jnp.where(group_of == group, picked[group * 16 : group * 16 + 16, :], 0.0)
    for c in range(3):
        send[c] = jnp.where(
            point == 0,
            total[3 * c : 3 * c + 1, :],
            jnp.where(point == 1, total[3 * c + 1 : 3 * c + 2, :], total[3 * c + 2 : 3 * c + 3, :]),
        )


def near_offset():
    return jnp.where(lax.axis_index("patch") % 2 == 0, 2, 0)


FAR_ROWS = 5
LOW_PAIRS = 5
HIGH_PAIR = 59


def ends_kernel(
    wide_a, wide_b, wide_c, near_rows, far_rows, points,
    field_in, operand_in, moving_in, outer_in, mass_in, thick_in, force_in, compact_in, table_in,
    field, operand, moving, outer, mass, thick, force, compact, table, send_far,
):
    even = lax.axis_index("patch") % 2 == 0
    put_halo(field, near_rows, far_rows, even, 0, 3)
    put_halo(moving, near_rows, far_rows, even, 384, 3)
    put_halo(outer, near_rows, far_rows, even, 768, 3)
    put_halo(mass, near_rows, far_rows, even, 1152, 1)
    put_halo(thick, near_rows, far_rows, even, 1280, 1)
    for step in list(range(6)) + list(range(60, 67)):
        fill_operand(field, operand, step)
    low = LOW_PAIRS * 16
    high = (PAIRS - HIGH_PAIR) * 16
    parts = [
        jnp.concatenate(
            [
                operand[i % 2, (i // 2) * 16 : (i // 2) * 16 + low, :],
                operand[i % 2, (HIGH_PAIR + i // 2) * 16 : (HIGH_PAIR + i // 2) * 16 + high, :],
            ],
            axis=0,
        )
        for i in range(6)
    ]
    results = pair_products(parts, wide_a, wide_b, wide_c)
    for half in range(2):
        for c in range(3):
            force[half, 0:low, cols(c)] = results[half][c][:low]
            force[half, HIGH_PAIR * 16 : PAIR_ROWS, cols(c)] = results[half][c][low:]
    for i, step in enumerate(list(range(LOW_PAIRS)) + list(range(HIGH_PAIR, PAIRS))):
        compact_rows(step, field, moving, thick, compact, some_rows(results, i))
    turn_rows(compact, table, [0, 15])
    pick_slots(points[2 - near_offset()], table, send_far)
    for c in range(3, FAR_ROWS):
        send_far[c] = jnp.zeros((1, SLOTS), F32)


def pick_kernel(table, points, stiffest, send_mid, send_near):
    send_near[3] = jnp.concatenate([stiffest[0:1, :]] * (SLOTS // 128), axis=1)
    pick_slots(points[near_offset()], table, send_near)
    pick_slots(points[1], table, send_mid)


def slot_weight(j, weights):
    neighbour = lax.axis_index("patch") + (j - 1)
    present = jnp.where((neighbour >= 0) & (neighbour < lax.axis_size("patch")), 1.0, 0.0)
    return weights[j] * present


def own_kernel(points, weights, compact, own, total):
    place = lax.broadcasted_iota(jnp.int32, (128, SLOTS), 0)
    line = lax.broadcasted_iota(jnp.int32, (16, SLOTS), 0)
    summed = None
    for j in range(3):
        group_of, low, point = slot_place(points[j])
        weight = slot_weight(j, weights)
        upper = weight.astype(BF16).astype(F32)
        both = jnp.where(line == point, upper, jnp.where(line == point + 8, weight - upper, 0.0)).astype(BF16)
        zero = jnp.zeros((16, SLOTS), BF16)
        right = jnp.concatenate([jnp.where(group_of == group, both, zero) for group in range(16)], axis=0)
        part = dot_nt(jnp.where(place == low, 1.0, 0.0).astype(BF16), right)
        summed = part if summed is None else summed + part
    total[...] = summed
    lane = lax.broadcasted_iota(jnp.int32, (128, 128), 1)
    for group in range(16):
        half = total[:, (group // 8) * 128 : (group // 8) * 128 + 128]
        half = half + pltpu.roll(half, 120, 1)
        shift = (group % 8) * 16
        weight_sum = jnp.where(
            lane < 3,
            pltpu.roll(half, 128 - shift, 1) if shift else half,
            jnp.where(
                lane < 6,
                pltpu.roll(half, (131 - shift) % 128, 1),
                pltpu.roll(half, (134 - shift) % 128, 1),
            ),
        )
        start = TOP + HALO + group * 128
        own[group * 128 : group * 128 + 128, :] = jnp.where(
            lane < 9, compact[start : start + 128, :] * weight_sum, 0.0
        )


def sum_slots(j, got, points, weights):
    place = lax.broadcasted_iota(jnp.int32, (128, SLOTS), 0)
    line = lax.broadcasted_iota(jnp.int32, (16, SLOTS), 0)
    group_of, low, point = slot_place(points[j])
    weight = slot_weight(j, weights)
    spread_out = jnp.zeros((16, SLOTS), F32)
    for c in range(3):
        spread_out = jnp.where(line == 3 * c + point, weight * got[c], spread_out)
    high = spread_out.astype(BF16)
    rest = (spread_out - high.astype(F32)).astype(BF16)
    zero = jnp.zeros((16, SLOTS), BF16)
    right = jnp.concatenate(
        [jnp.where(group_of == group, high, zero) for group in range(16)]
        + [jnp.where(group_of == group, rest, zero) for group in range(16)],
        axis=0,
    )
    chosen = jnp.where(place == low, 1.0, 0.0).astype(BF16)
    part = dot_nt(chosen, right)
    return part[:, 0:256] + part[:, 256:512]


def half_couple_kernel(got_mid, got_near, points, weights, stiffest, partial, most):
    partial[...] = sum_slots(1, got_mid, points, weights) + sum_slots(near_offset(), got_near, points, weights)
    most[...] = jnp.maximum(stiffest[...], jnp.broadcast_to(got_near[3][:, 0:128], (8, 128)))


def couple_kernel(got_far, points, weights, partial, most, own, coupling, parcel, total):
    block = lax.axis_index("patch")
    blocks = lax.axis_size("patch")
    total[...] = partial[...] + sum_slots(2 - near_offset(), got_far, points, weights)
    lane = lax.broadcasted_iota(jnp.int32, (128, 128), 1)
    edges = []
    for group in range(16):
        half = total[:, (group // 8) * 128 : (group // 8) * 128 + 128]
        shift = (group % 8) * 16
        block_sum = pltpu.roll(half, 128 - shift, 1) if shift else half
        start = TOP + HALO + group * 128
        here = jnp.where(lane < 9, block_sum, 0.0) - own[group * 128 : group * 128 + 128, :]
        coupling[start : start + 128, :] = here
        if group == 0:
            edges.append(here[0:8, :])
        if group == 15:
            edges.append(here[120:128, :])
    lane_row = lax.broadcasted_iota(jnp.int32, (1, 128), 1)
    flat = []
    for edge in edges:
        line_up = edge[0:1, :]
        for row in range(1, 8):
            line_up = line_up + pltpu.roll(edge, 16 * row, 1)[row : row + 1, :]
        flat.append(jnp.where(lane_row == 15, most[0:1, :], line_up))
    parcel[...] = jnp.broadcast_to(flat[0][None], (blocks, 1, 128))
    parcel[jnp.minimum(block + 1, blocks - 1)] = flat[1]


def step_kernel(
    parcel, field, moving, outer, mass, thick, force, coupling_in, wide_a, wide_b, wide_c,
    new_field, new_moving, couple,
    state, speed, push, drag, operand_a, operand_b, place_out, speed_out, place_late, speed_late, sem_out, sem_late,
):
    block = lax.axis_index("patch")
    blocks = lax.axis_size("patch")
    fine = lax.axis_index("grp") == 1
    lane_row = lax.broadcasted_iota(jnp.int32, (1, 128), 1)
    sublane = lax.broadcasted_iota(jnp.int32, (8, 128), 0)
    most = jnp.max(parcel[...].reshape(blocks, 128), axis=0, keepdims=True)
    most = jnp.max(jnp.where(lane_row == 15, most, 0.0), axis=1, keepdims=True)
    limit = jnp.broadcast_to(most, (16, 128))
    base_step = COURANT * (1.0 / jnp.sqrt(limit))
    size = jnp.where(fine, base_step, SUBSTEPS * base_step)
    square = size * size
    inverse = 1.0 / size
    for start, there, exists in [
        (TOP, jnp.maximum(block - 1, 0), block > 0),
        (TOP + HALO + ROWS, jnp.minimum(block + 1, blocks - 1), block < blocks - 1),
    ]:
        line_up = jnp.broadcast_to(parcel[there], (8, 128))
        edge = line_up
        for row in range(1, 8):
            edge = jnp.where(sublane == row, pltpu.roll(line_up, 128 - 16 * row, 1), edge)
        edge = jnp.where(lax.broadcasted_iota(jnp.int32, (8, 128), 1) < 9, edge, 0.0)
        couple[start : start + 8, :] = jnp.where(exists, edge, 0.0)
    couple[0:TOP, :] = jnp.zeros((TOP, 128), F32)
    couple[PLANE - 8 : PLANE, :] = jnp.zeros((8, 128), F32)
    lane = lax.broadcasted_iota(jnp.int32, (16, 128), 1)

    def first_update(step, keep):
        for half in range(2):
            at = spread(2 * step + half)
            tile = pl.ds(step * 16, 16) if isinstance(step, int) else pl.ds(pl.multiple_of(step * 16, 16), 16)
            scaled = square * mass[0, at, :]
            pull = scaled * thick[0, at, :]
            both = couple[at, :]
            if keep:
                drag[half, tile, :] = pull
            for c in range(3):
                here = jnp.where(lane < 3, pltpu.roll(both, 128 - 3 * c, 1) if c else both, 0.0)
                drive = scaled * (outer[c, at, :] + here)
                new_speed = size * moving[c, at, :] + (drive - pull * force[half, tile, cols(c)])
                place = field[c, at, :] + new_speed
                if keep:
                    push[half, tile, cols(c)] = drive
                    speed[half, tile, cols(c)] = new_speed
                    state[half, tile, cols(c)] = place
                    operand_a[half, step * 16 + 16 : step * 16 + 32, cols(c)] = place.astype(BF16)
                else:
                    place_out[c, at, :] = place
                    speed_out[c, at, :] = new_speed * inverse

    @pl.when(jnp.logical_not(fine))
    def _():
        def some(turn, carry):
            for i in range(5):
                first_update(turn * 5 + i, False)
            return carry

        lax.fori_loop(0, PAIRS // 5, some, 0)
        out = []
        for c in range(3):
            inner = pl.ds(TOP + HALO, ROWS)
            out.append(
                pltpu.make_async_copy(place_out.at[c, inner, :], new_field.at[0, :, pl.ds(c * 128, 128)], sem_out.at[c])
            )
            out.append(
                pltpu.make_async_copy(speed_out.at[c, inner, :], new_moving.at[0, :, pl.ds(c * 128, 128)], sem_out.at[3 + c])
            )
        for copy in out:
            copy.start()
        for copy in out:
            copy.wait()

    def low_ends(operand):
        for c in range(3):
            operand[0, 0:16, cols(c)] = pltpu.roll(state[1, 63 * 16 : 64 * 16, cols(c)], 1, 0).astype(BF16)
            operand[1, 0:16, cols(c)] = pltpu.roll(state[0, 64 * 16 : 65 * 16, cols(c)], 1, 0).astype(BF16)

    def high_ends(operand):
        for c in range(3):
            operand[0, 66 * 16 : 67 * 16, cols(c)] = pltpu.roll(state[1, 0:16, cols(c)], 15, 0).astype(BF16)
            operand[1, 66 * 16 : 67 * 16, cols(c)] = pltpu.roll(state[0, 16:32, cols(c)], 15, 0).astype(BF16)

    def update(chunk, results, following):
        start = chunk * CHUNK
        rows = slice(start, start + CHUNK)
        for half in range(2):
            pull = drag[half, rows, :]
            for c in range(3):
                new_speed = speed[half, rows, cols(c)] + (push[half, rows, cols(c)] - pull * results[half][c])
                place = state[half, rows, cols(c)] + new_speed
                if following is not None:
                    speed[half, rows, cols(c)] = new_speed
                    state[half, rows, cols(c)] = place
                    following[half, start + 16 : start + 16 + CHUNK, cols(c)] = place.astype(BF16)
                else:
                    for i in range(CHUNK_PAIRS):
                        k = 2 * (start // 16 + i) + half
                        some_place = place[i * 16 : i * 16 + 16, :]
                        some_speed = new_speed[i * 16 : i * 16 + 16, :] * inverse
                        if k >= EARLY:
                            place_out[c, spread(k), :] = some_place
                            speed_out[c, spread(k), :] = some_speed
                        if k < EARLY + 8 or RUN - 9 <= k < RUN:
                            place_late[c, spread(k), :] = some_place
                            speed_late[c, spread(k), :] = some_speed
        if following is not None and chunk == 0:
            high_ends(following)
        if following is not None and chunk == PAIR_ROWS // CHUNK - 1:
            low_ends(following)

    @pl.when(fine)
    def _():
        for step in [63, 64] + list(range(CHUNK_PAIRS + 1)):
            first_update(step, True)
        low_ends(operand_a)
        high_ends(operand_a)
        pieces = []
        done = 0
        for run in range(16):
            begin = (run * RUN + EARLY - HALO + 7) // 8 * 8
            end = min((run * RUN + RUN - HALO) // 8 * 8, ROWS)
            pieces.append((done, begin, end))
            done = end
        assert done == ROWS
        targets = [(place_out, place_late, new_field), (speed_out, speed_late, new_moving)]

        def copies(late, rows):
            made = []
            for i, pair in enumerate(targets):
                for c in range(3):
                    for first, count in rows:
                        made.append(
                            pltpu.make_async_copy(
                                pair[late].at[c, pl.ds(TOP + HALO + first, count), :],
                                pair[2].at[0, pl.ds(first, count), pl.ds(c * 128, 128)],
                                (sem_late if late else sem_out).at[3 * i + c],
                            )
                        )
            return made

        early_rows = [(begin, end - begin) for _, begin, end in pieces]
        late_rows = [(gap, begin - gap) for gap, begin, _ in pieces]
        before = None
        for operand, following, order in [
            (operand_a, operand_b, [0, 1, 2, 3, 4]),
            (operand_b, operand_a, [1, 2, 3, 4, 0]),
            (operand_a, None, [2, 3, 4, 0, 1]),
        ]:
            for chunk in order:
                results = band_products(operand, chunk * CHUNK, CHUNK, wide_a, wide_b, wide_c)
                if operand is operand_a and following is operand_b:
                    first = (chunk + 1) * CHUNK_PAIRS + 1
                    for step in range(first, min(first + CHUNK_PAIRS, 63)):
                        first_update(step, True)
                if before is not None:
                    update(*before)
                    if before[0] == 4 and before[2] is None:
                        for copy in copies(0, early_rows):
                            copy.start()
                before = (chunk, results, following)
        update(*before)
        for copy in copies(1, late_rows):
            copy.start()
        for late, rows in enumerate([early_rows, late_rows]):
            for copy in copies(late, [(0, sum(count for _, count in rows))]):
                copy.wait()


ANY = pl.BlockSpec(memory_space=pl.ANY)
IN_VMEM = pl.BlockSpec(memory_space=pltpu.VMEM)
DMA = pltpu.SemaphoreType.DMA
PLANE_3 = pltpu.VMEM((3, PLANE, 128), F32)
PLANE_1 = pltpu.VMEM((1, PLANE, 128), F32)
FULL = pltpu.VMEM((2, PAIR_ROWS, ROW), F32)
OPERAND = pltpu.VMEM((2, BAND_ROWS, ROW), BF16)
BANDS = [
    pltpu.VMEM((5 * ROW, 256), BF16),
    pltpu.VMEM((6 * ROW, 256), BF16),
    pltpu.VMEM((5 * ROW, 256), BF16),
]


def near(*arrays):
    return [pltpu.with_memory_space_constraint(a, pltpu.VMEM) for a in arrays]


def params(mib):
    return pltpu.CompilerParams(vmem_limit_bytes=mib * 2**20)


def per_device(
    displace, velocity, ext_force, inv_mass, thickness, stiff_bands, pair_points, pair_weights
):
    blocks = lax.axis_size("patch")
    points = pair_points.reshape(3, 1, SLOTS)
    weights = pair_weights.reshape(3, 1, SLOTS)
    near_pairs = [(i, i ^ 1) for i in range(blocks)]
    far_pairs = [(i, i + 1 if i % 2 else i - 1) for i in range(1, blocks - 1)]
    width = 3 * ROW + 2 * POINTS
    near_rows, far_rows = pl.pallas_call(
        bundle_kernel,
        out_shape=(pltpu.VMEM((HALO, width), F32), pltpu.VMEM((HALO, width), F32)),
        in_specs=[ANY] * 5,
        out_specs=[IN_VMEM] * 2,
        scratch_shapes=[DMA((10,))],
        compiler_params=params(2),
        name="bundle",
    )(*[pltpu.with_memory_space_constraint(a, pltpu.HBM) for a in [displace, velocity, ext_force, inv_mass, thickness]])
    far_rows = lax.ppermute(far_rows, "patch", far_pairs)

    field, operand, *bands, near_rows = pl.pallas_call(
        load_kernel,
        out_shape=(PLANE_3, OPERAND, *BANDS, pltpu.VMEM((HALO, width), F32)),
        in_specs=[ANY] * 2 + [IN_VMEM],
        out_specs=[IN_VMEM] * 6,
        input_output_aliases={2: 5},
        scratch_shapes=[DMA((3,)), DMA((20,))],
        compiler_params=params(2),
        name="load",
    )(displace, stiff_bands, *near(near_rows))
    near_rows = lax.ppermute(near_rows, "patch", near_pairs)

    plane = pltpu.VMEM((PLANE, 128), F32)
    tile = pltpu.VMEM((8, 128), F32)
    table = pltpu.VMEM((256, 256), BF16)
    moving, outer, mass, thick, force, compact, stiffest, turned = pl.pallas_call(
        force_kernel,
        out_shape=(PLANE_3, PLANE_3, PLANE_1, PLANE_1, FULL, plane, tile, table),
        in_specs=[IN_VMEM] * 5 + [ANY] * 4,
        out_specs=[IN_VMEM] * 8,
        scratch_shapes=[DMA((3,)), DMA((3,)), DMA((1,)), DMA((1,))],
        compiler_params=params(12),
        name="force",
    )(*near(field, operand, *bands), velocity, ext_force, inv_mass, thickness)

    slots = pltpu.VMEM((3, 1, SLOTS), F32)
    field, operand, moving, outer, mass, thick, force, compact, table, send_far = pl.pallas_call(
        ends_kernel,
        out_shape=(PLANE_3, OPERAND, PLANE_3, PLANE_3, PLANE_1, PLANE_1, FULL, plane, table, pltpu.VMEM((FAR_ROWS, 1, SLOTS), F32)),
        in_specs=[IN_VMEM] * 15,
        out_specs=[IN_VMEM] * 10,
        input_output_aliases={i + 6: i for i in range(9)},
        compiler_params=params(12),
        name="ends",
    )(*near(*bands, near_rows, far_rows, points, field, operand, moving, outer, mass, thick, force, compact, turned))

    both = ("grp", "patch")
    mid_pairs = [(i, i) for i in range(blocks)]

    def across(send, pairs):
        return lax.ppermute(
            send, both, [(g * blocks + i, (1 - g) * blocks + t) for g in range(2) for i, t in pairs]
        )

    got_far = across(send_far, far_pairs)
    send_mid, send_near = pl.pallas_call(
        pick_kernel,
        out_shape=(slots, pltpu.VMEM((4, 1, SLOTS), F32)),
        in_specs=[IN_VMEM] * 3,
        out_specs=[IN_VMEM] * 2,
        compiler_params=params(12),
        cost_estimate=pl.CostEstimate(flops=1, transcendentals=0, bytes_accessed=1),
        name="pick",
    )(*near(table, points, stiffest))
    got_mid = across(send_mid, mid_pairs)
    got_near = across(send_near, near_pairs)
    own = pl.pallas_call(
        own_kernel,
        out_shape=pltpu.VMEM((ROWS, 128), F32),
        in_specs=[IN_VMEM] * 3,
        out_specs=IN_VMEM,
        scratch_shapes=[pltpu.VMEM((128, 256), F32)],
        compiler_params=params(12),
        name="own",
    )(*near(points, weights, compact))
    partial, most = pl.pallas_call(
        half_couple_kernel,
        out_shape=(pltpu.VMEM((128, 256), F32), tile),
        in_specs=[IN_VMEM] * 5,
        out_specs=[IN_VMEM] * 2,
        compiler_params=params(12),
        cost_estimate=pl.CostEstimate(flops=1, transcendentals=0, bytes_accessed=1),
        name="half_couple",
    )(*near(got_mid, got_near, points, weights, stiffest))
    coupling, parcel = pl.pallas_call(
        couple_kernel,
        out_shape=(plane, pltpu.VMEM((blocks, 1, 128), F32)),
        in_specs=[IN_VMEM] * 6,
        out_specs=[IN_VMEM] * 2,
        scratch_shapes=[pltpu.VMEM((128, 256), F32)],
        compiler_params=params(12),
        name="couple",
    )(*near(got_far, points, weights, partial, most, own))
    parcel = lax.all_to_all(parcel, "patch", 0, 0)

    new_field, new_moving, unused = pl.pallas_call(
        step_kernel,
        out_shape=(
            jax.ShapeDtypeStruct((1, ROWS, ROW), F32),
            jax.ShapeDtypeStruct((1, ROWS, ROW), F32),
            pltpu.VMEM((PLANE, 128), F32),
        ),
        in_specs=[IN_VMEM] * 11,
        out_specs=[ANY] * 2 + [IN_VMEM],
        input_output_aliases={7: 2},
        scratch_shapes=[FULL, FULL, FULL, pltpu.VMEM((2, PAIR_ROWS, 128), F32)]
        + [OPERAND, OPERAND, PLANE_3, PLANE_3, PLANE_3, PLANE_3, DMA((6,)), DMA((6,))],
        compiler_params=params(35),
        name="steps",
    )(*near(parcel, field, moving, outer, mass, thick, force, coupling, *bands))
    return new_field, new_moving


def solution(mesh):
    spec3 = P("grp", "patch", None)
    spec4 = P("grp", "patch", None, None)
    return jax.shard_map(
        per_device,
        mesh=mesh,
        in_specs=(spec3, spec3, spec3, spec3, spec3, P(), spec4, spec4),
        out_specs=(spec3, spec3),
        check_vma=False,
    )
```
